32 devices in a mesh: dp: 16 (over z, x, core), tensor: 2 (over y).
Axes of the slice: x: 2, y: 2, z: 4, core: 2. Of those that a mesh axis runs over, the one named last changes fastest.
Arguments:
- block_input: bfloat16 [3072, 1024], P('dp'), may hold values from -6 to 6
- cotangent: bfloat16 [3072, 1024], P('dp'), may hold values from -6 to 6
- seq_len: int32 [48], P('dp'), may hold values from 0 to 64, as said below
- norm_gain: bfloat16 [2, 1024], P(None, 'dp'), may hold values from 0.5 to 1.5
- gate_inner_proj: bfloat16 [2, 1024, 2, 2048], P(None, 'dp', None, 'tensor'), may hold values from -0.1875 to 0.1875
- step_proj: bfloat16 [2, 1024, 32], P(None, 'dp', 'tensor'), may hold values from -0.1875 to 0.1875
- state_proj: bfloat16 [2, 1024, 256], P(None, 'dp'), may hold values from -0.1875 to 0.1875
- conv_inner: bfloat16 [2, 4, 2048], P(None, None, ('tensor', 'dp')), may hold values from -3 to 3
- conv_inner_bias: bfloat16 [2, 2048], P(None, ('tensor', 'dp')), may hold values from -3 to 3
- conv_state: bfloat16 [2, 4, 256], P(None, None, 'dp'), may hold values from -3 to 3
- conv_state_bias: bfloat16 [2, 256], P(None, 'dp'), may hold values from -3 to 3
- step_bias: bfloat16 [2, 32], P(None, 'tensor'), may hold values from -6 to -2
- log_rate: bfloat16 [2, 32], P(None, 'tensor'), may hold values from 0 to 2.796875
- skip_gain: bfloat16 [2, 32], P(None, 'tensor'), may hold values from 0.5 to 1.5
- gate_gain: bfloat16 [2, 2048], P(None, ('tensor', 'dp')), may hold values from 0.5 to 1.5
- out_proj: bfloat16 [2, 2048, 1024], P(None, 'tensor', 'dp'), may hold values from -0.125 to 0.125
Outputs:
- block_out: bfloat16 [3072, 1024], P('dp')
- grad_input: bfloat16 [3072, 1024], P('dp')
- grad_norm_gain: float32 [2, 1024], P(None, 'dp')
- grad_gate_inner_proj: float32 [2, 1024, 2, 2048], P(None, 'dp', None, 'tensor')
- grad_step_proj: float32 [2, 1024, 32], P(None, 'dp', 'tensor')
- grad_state_proj: float32 [2, 1024, 256], P(None, 'dp')
- grad_conv_inner: float32 [2, 4, 2048], P(None, None, ('tensor', 'dp'))
- grad_conv_inner_bias: float32 [2, 2048], P(None, ('tensor', 'dp'))
- grad_conv_state: float32 [2, 4, 256], P(None, None, 'dp')
- grad_conv_state_bias: float32 [2, 256], P(None, 'dp')
- grad_step_bias: float32 [2, 32], P(None, 'tensor')
- grad_log_rate: float32 [2, 32], P(None, 'tensor')
- grad_skip_gain: float32 [2, 32], P(None, 'tensor')
- grad_gate_gain: float32 [2, 2048], P(None, ('tensor', 'dp'))
- grad_out_proj: float32 [2, 2048, 1024], P(None, 'tensor', 'dp')
The draws below stay inside these ranges and needn't reach their ends.
Inputs may be any that keep to these rules, and one draw needn't show every extreme that they name: `seq_len`: indices d and d + 8 of dp form a pair: in each pair one index has all 3 lengths at least 32, and the pair's 3 + 3 lengths sum to at most 192; some length equals 64.
All inputs are finite; a program needn't handle non-finite values.
Results may differ from the reference program's by a relative error of at most 0.015.
Values may be sent and summed in bfloat16 or wider, within the bound.
A program may use at most 192 MiB of HBM per device.

```python
import jax
import jax.numpy as jnp
from jax import lax

D = 1024
H = 32
N = 128
E = 2048
KERNEL = 4
LAYERS = 2
SPD = 3
LMAX = 64
ROWS_IN = 192
BAL = 128
TOKENS_IN = 3072
N_DP = 16


def draw_seq_len(key, part):
    half_axis = N_DP // 2
    key_heavy, key_light, key_side = jax.random.split(key, 3)
    heavy_len = jax.random.randint(key_heavy, (half_axis, SPD), LMAX // 2, LMAX + 1, dtype=jnp.int32)
    heavy_len = heavy_len.at[0, 0].set(LMAX)
    spare_room = (SPD * LMAX - jnp.sum(heavy_len, axis=1)) // SPD
    light_len = jax.random.randint(key_light, (half_axis, SPD), 0, spare_room[:, None] + 1, dtype=jnp.int32)
    heavy_side = jax.random.randint(key_side, (half_axis, 1), 0, 2, dtype=jnp.int32)
    lower_half = jnp.where(heavy_side == 1, heavy_len, light_len)
    upper_half = jnp.where(heavy_side == 1, light_len, heavy_len)
    return jnp.concatenate([lower_half, upper_half], axis=0).reshape(N_DP * SPD).astype(jnp.int32)


def levels(key, extent, cuts, smallest, high):
    loudness = 1.0
    for axis_at, parts in cuts:
        steps = jax.random.uniform(jax.random.fold_in(jax.random.fold_in(key, 6), axis_at), (parts,), jnp.float32, smallest / len(cuts), high / len(cuts))
        loudness = loudness * jnp.repeat(jnp.exp(steps), extent[axis_at] // parts).reshape((-1,) + (1,) * (len(extent) - 1 - axis_at))
    return loudness


def scatter_about(rng, extent, spread, bound, pieces=(), held_as=jnp.bfloat16):
    factor_of = levels(rng, extent, pieces, -0.22, 0.18) if pieces else 1.0
    array = jax.random.normal(rng, extent, jnp.float32) * spread * factor_of
    return jnp.minimum(jnp.maximum(array, -bound), bound).astype(held_as)


def setup_inputs(seed: int = 0) -> dict:
    keys = jax.random.split(jax.random.key(seed), 17)
    return {
        "block_input": scatter_about(keys[0], (TOKENS_IN, D), 1.0, 6.0, ((0, 16),)),
        "cotangent": scatter_about(keys[1], (TOKENS_IN, D), 1.0, 6.0, ((0, 16),)),
        "seq_len": draw_seq_len(jax.random.fold_in(keys[16], 71), 0),
        "norm_gain": jnp.clip(1.0 + 0.1 * jax.random.normal(keys[3], (LAYERS, D), jnp.float32), 0.5, 1.5).astype(jnp.bfloat16),
        "gate_inner_proj": scatter_about(keys[4], (LAYERS, D, 2, E), D ** -0.5, 0.1875, ((1, 16), (3, 2))),
        "step_proj": scatter_about(keys[5], (LAYERS, D, H), D ** -0.5, 0.1875, ((1, 16), (2, 2))),
        "state_proj": scatter_about(keys[6], (LAYERS, D, 2 * N), D ** -0.5, 0.1875, ((1, 16),)),
        "conv_inner": scatter_about(keys[7], (LAYERS, KERNEL, E), KERNEL ** -0.5, 3.0, ((2, 32),)),
        "conv_inner_bias": scatter_about(keys[8], (LAYERS, E), 0.5, 3.0, ((1, 32),)),
        "conv_state": scatter_about(keys[9], (LAYERS, KERNEL, 2 * N), KERNEL ** -0.5, 3.0, ((2, 16),)),
        "conv_state_bias": scatter_about(keys[10], (LAYERS, 2 * N), 0.5, 3.0, ((1, 16),)),
        "step_bias": jnp.clip(-6.0 + 4.0 * jax.random.uniform(keys[11], (LAYERS, H), jnp.float32) ** levels(keys[11], (LAYERS, H), ((1, 2),), -0.2, 0.2), -6.0, -2.0).astype(jnp.bfloat16),
        "log_rate": jnp.clip(2.796875 * jax.random.uniform(keys[12], (LAYERS, H), jnp.float32) ** levels(keys[12], (LAYERS, H), ((1, 2),), -0.2, 0.2), 0.0, 2.796875).astype(jnp.bfloat16),
        "skip_gain": jnp.clip(0.5 + 1.0 * jax.random.uniform(keys[13], (LAYERS, H), jnp.float32) ** levels(keys[13], (LAYERS, H), ((1, 2),), -0.2, 0.2), 0.5, 1.5).astype(jnp.bfloat16),
        "gate_gain": jnp.clip(1.0 + 0.1 * jax.random.normal(keys[14], (LAYERS, E), jnp.float32), 0.5, 1.5).astype(jnp.bfloat16),
        "out_proj": scatter_about(keys[15], (LAYERS, E, D), E ** -0.5, 0.125, ((1, 2), (2, 16))),
    }


EPSILON = 1e-05
HIGHEST = lax.Precision.HIGHEST

def shifted(values, lag_rows):
    padding = jnp.zeros((lag_rows,) + values.shape[1:], values.dtype)
    return jnp.concatenate([padding, values[:-lag_rows]], axis=0)

def unshifted(values, lag_rows):
    padding = jnp.zeros((lag_rows,) + values.shape[1:], values.dtype)
    return jnp.concatenate([values[lag_rows:], padding], axis=0)

def silu_slope(values):
    sigmoid_val = jax.nn.sigmoid(values)
    return sigmoid_val * (1.0 + values * (1.0 - sigmoid_val))

def segments_of(lengths, row_total):
    ends = jnp.cumsum(lengths).astype(jnp.int32)
    position = jnp.arange(row_total, dtype=jnp.int32)
    return lax.optimization_barrier(jnp.sum((position[:, None] >= ends[None, :]).astype(jnp.int32), axis=1)).astype(jnp.int32)

def seq_structure(segment_ids):
    row_total = segment_ids.shape[0]
    position = jnp.arange(row_total, dtype=jnp.int32)
    same_seq = ((segment_ids[:, None] == segment_ids[None, :]) & (position[:, None] >= position[None, :])).astype(jnp.float32)
    conv_masks = [None]
    for lag_rows in range(1, KERNEL):
        earlier = jnp.concatenate([jnp.full((lag_rows,), -1, jnp.int32), segment_ids[:-lag_rows]])
        conv_masks.append((segment_ids == earlier).astype(jnp.float32)[:, None])
    return (same_seq, conv_masks)

def conv_apply(source, kernel, bias_vec, conv_masks):
    tap_count = kernel.shape[0]
    result = bias_vec[None, :] + kernel[tap_count - 1][None, :] * source
    for lag_rows in range(1, tap_count):
        result = result + kernel[tap_count - 1 - lag_rows][None, :] * shifted(source, lag_rows) * conv_masks[lag_rows]
    return result

def conv_back(grad_pre, source, kernel, conv_masks):
    tap_count = kernel.shape[0]
    tap_grads = []
    grad_source = kernel[tap_count - 1][None, :] * grad_pre
    for tap_index in range(tap_count):
        lag_rows = tap_count - 1 - tap_index
        if lag_rows == 0:
            tap_grads.append(lax.optimization_barrier(jnp.sum(grad_pre * source, axis=0)))
        else:
            masked = grad_pre * conv_masks[lag_rows]
            tap_grads.append(lax.optimization_barrier(jnp.sum(masked * shifted(source, lag_rows), axis=0)))
            grad_source = grad_source + kernel[tap_index][None, :] * unshifted(masked, lag_rows)
    return (jnp.stack(tap_grads), lax.optimization_barrier(jnp.sum(grad_pre, axis=0)), grad_source)

def decay_matrix(cum_decay, same_seq):
    diff = cum_decay.T[:, :, None] - cum_decay.T[:, None, :]
    inside = same_seq[None, :, :] > 0.5
    return jnp.where(inside, jnp.exp(jnp.where(inside, diff, 0.0)), 0.0)

def take_rows(buffer, start_row, row_count):
    padding = jnp.zeros((row_count, buffer.shape[1]), buffer.dtype)
    return lax.dynamic_slice_in_dim(jnp.concatenate([buffer, padding], axis=0), start_row, row_count, 0)

def place_rows(own_rows, arrived, kept_rows, rows_out):
    row_width = own_rows.shape[1]
    if own_rows.shape[0] >= rows_out:
        base_rows = own_rows[:rows_out]
    else:
        base_rows = jnp.concatenate([own_rows, jnp.zeros((rows_out - own_rows.shape[0], row_width), own_rows.dtype)], axis=0)
    extended = jnp.concatenate([jnp.zeros((rows_out, row_width), own_rows.dtype), arrived, jnp.zeros((rows_out - arrived.shape[0], row_width), own_rows.dtype)], axis=0)
    moved_rows = lax.dynamic_slice_in_dim(extended, (rows_out - kept_rows).astype(jnp.int32), rows_out, 0)
    position = jnp.arange(rows_out, dtype=jnp.int32)
    return jnp.where((position < kept_rows)[:, None], base_rows, moved_rows)

def balanced_layout(own_len, partner_len):
    own_end = jnp.cumsum(own_len).astype(jnp.int32)
    keep_flag = (own_end <= BAL).astype(jnp.int32)
    kept_rows = jnp.sum(own_len * keep_flag).astype(jnp.int32)
    partner_end = jnp.cumsum(partner_len).astype(jnp.int32)
    incoming = (partner_len * (partner_end > BAL).astype(jnp.int32)).astype(jnp.int32)
    segment_ids = segments_of(jnp.concatenate([own_len * keep_flag, incoming]).astype(jnp.int32), BAL)
    live_rows = (jnp.arange(BAL, dtype=jnp.int32) < kept_rows + jnp.sum(incoming).astype(jnp.int32))[:, None]
    return (segment_ids, live_rows, kept_rows)

def forward_layer(stream, gathered, head_vals, same_seq, conv_masks):
    gate_inner, step_weight, state_weight, conv_inner, conv_inner_bias, conv_state, conv_state_bias, norm_gain, gate_gain, out_weight = gathered
    step_bias, log_rate, skip_gain = head_vals
    inv_rms = lax.rsqrt(lax.optimization_barrier(jnp.mean(stream * stream, axis=1, keepdims=True)) + EPSILON)
    normed = (stream * inv_rms * norm_gain.astype(jnp.float32)[None, :]).astype(jnp.bfloat16)
    model_rows, gate_pair, inner_width = gate_inner.shape
    joined = jnp.dot(normed, gate_inner.reshape(model_rows, gate_pair * inner_width), preferred_element_type=jnp.float32)
    gate_pre = joined[:, :inner_width]
    inner_raw = joined[:, inner_width:]
    step_raw = jnp.dot(normed, step_weight, preferred_element_type=jnp.float32)
    state_raw = jnp.dot(normed, state_weight, preferred_element_type=jnp.float32)
    inner_pre = conv_apply(inner_raw, conv_inner.astype(jnp.float32), conv_inner_bias.astype(jnp.float32), conv_masks)
    state_pre = conv_apply(state_raw, conv_state.astype(jnp.float32), conv_state_bias.astype(jnp.float32), conv_masks)
    inner_act = jax.nn.silu(inner_pre)
    state_act = jax.nn.silu(state_pre)
    half_state = state_act.shape[1] // 2
    state_in = state_act[:, :half_state]
    state_out = state_act[:, half_state:]
    step_size = jax.nn.softplus(step_raw + step_bias[None, :])
    decay_rate = -jnp.exp(log_rate)
    cum_decay = jnp.dot(same_seq, step_size * decay_rate[None, :], precision=HIGHEST)
    decay_mat = decay_matrix(cum_decay, same_seq)
    intersection = jnp.dot(state_out, state_in.T, precision=HIGHEST)
    total_rows, head_count = step_size.shape
    inner_heads = inner_act.reshape(total_rows, head_count, -1)
    scaled_in = inner_heads * step_size[:, :, None]
    mixer_mat = decay_mat * intersection[None]
    ssm_heads = jnp.einsum('hts,shp->thp', mixer_mat, scaled_in, precision=HIGHEST) + skip_gain[None, :, None] * inner_heads
    ssm_out = ssm_heads.reshape(total_rows, -1)
    gate_sig = jax.nn.sigmoid(gate_pre)
    gated_out = ssm_out * gate_pre * gate_sig
    square_sum = lax.optimization_barrier(jnp.sum(gated_out * gated_out, axis=1))
    inv_gate = lax.rsqrt(square_sum / ssm_out.shape[1] + EPSILON)[:, None]
    gate_normed = (gated_out * inv_gate * gate_gain.astype(jnp.float32)[None, :]).astype(jnp.bfloat16)
    mixed = jnp.dot(gate_normed, out_weight, preferred_element_type=jnp.float32)
    kept_acts = (stream, inv_rms, normed, gate_pre, gate_sig, inner_raw, inner_pre, state_raw, state_pre, state_in, state_out, step_raw, step_size, decay_rate, decay_mat, intersection, inner_heads, scaled_in, ssm_out, gated_out, inv_gate, gate_normed)
    return (stream + mixed, kept_acts)

def backward_layer(gradient, gathered, head_vals, kept_acts, same_seq, conv_masks):
    gate_inner, step_weight, state_weight, conv_inner, conv_inner_bias, conv_state, conv_state_bias, norm_gain, gate_gain, out_weight = gathered
    step_bias, log_rate, skip_gain = head_vals
    stream, inv_rms, normed, gate_pre, gate_sig, inner_raw, inner_pre, state_raw, state_pre, state_in, state_out, step_raw, step_size, decay_rate, decay_mat, intersection, inner_heads, scaled_in, ssm_out, gated_out, inv_gate, gate_normed = kept_acts
    grad_low = gradient.astype(jnp.bfloat16)
    grad_out = jnp.dot(gate_normed.T, grad_low, preferred_element_type=jnp.float32)
    d_gate_normed = jnp.dot(grad_low, out_weight.T, preferred_element_type=jnp.float32)
    grad_gate_gain = lax.optimization_barrier(jnp.sum(d_gate_normed * gated_out * inv_gate, axis=0))
    scaled_grad = d_gate_normed * gate_gain.astype(jnp.float32)[None, :]
    inner_sum = lax.optimization_barrier(jnp.sum(scaled_grad * gated_out, axis=1))[:, None]
    d_gated = inv_gate * scaled_grad - gated_out * inv_gate ** 3 * inner_sum / ssm_out.shape[1]
    d_ssm = d_gated * gate_pre * gate_sig
    d_gate_pre = d_gated * ssm_out * gate_sig * (1.0 + gate_pre * (1.0 - gate_sig))
    d_heads = d_ssm.reshape(inner_heads.shape)
    grad_skip = lax.optimization_barrier(jnp.sum(d_heads * inner_heads, axis=(0, 2)))
    mixer_mat = decay_mat * intersection[None]
    d_scaled = jnp.einsum('hts,thp->shp', mixer_mat, d_heads, precision=HIGHEST)
    d_mixer = jnp.einsum('thp,shp->hts', d_heads, scaled_in, precision=HIGHEST)
    d_intersection = lax.optimization_barrier(jnp.sum(d_mixer * decay_mat, axis=0))
    flow_mat = d_mixer * mixer_mat
    d_cum = (lax.optimization_barrier(jnp.sum(flow_mat, axis=2)) - lax.optimization_barrier(jnp.sum(flow_mat, axis=1))).T
    d_log_decay = jnp.dot(same_seq.T, d_cum, precision=HIGHEST)
    d_inner_heads = skip_gain[None, :, None] * d_heads + d_scaled * step_size[:, :, None]
    d_step = lax.optimization_barrier(jnp.sum(d_scaled * inner_heads, axis=2)) + d_log_decay * decay_rate[None, :]
    grad_log_rate = lax.optimization_barrier(jnp.sum(d_log_decay * step_size, axis=0)) * decay_rate
    d_state_out = jnp.dot(d_intersection, state_in, precision=HIGHEST)
    d_state_in = jnp.dot(d_intersection.T, state_out, precision=HIGHEST)
    d_step_raw = d_step * jax.nn.sigmoid(step_raw + step_bias[None, :])
    grad_step_bias = lax.optimization_barrier(jnp.sum(d_step_raw, axis=0))
    d_state_act = jnp.concatenate([d_state_in, d_state_out], axis=1)
    d_inner_pre = d_inner_heads.reshape(inner_pre.shape) * silu_slope(inner_pre)
    d_state_pre = d_state_act * silu_slope(state_pre)
    grad_conv_inner, grad_conv_inner_bias, d_inner_raw = conv_back(d_inner_pre, inner_raw, conv_inner.astype(jnp.float32), conv_masks)
    grad_conv_state, grad_conv_state_bias, d_state_raw = conv_back(d_state_pre, state_raw, conv_state.astype(jnp.float32), conv_masks)
    d_joined = jnp.concatenate([d_gate_pre, d_inner_raw], axis=1).astype(jnp.bfloat16)
    d_step_low = d_step_raw.astype(jnp.bfloat16)
    d_state_low = d_state_raw.astype(jnp.bfloat16)
    model_rows, gate_pair, inner_width = gate_inner.shape
    joined_weight = gate_inner.reshape(model_rows, gate_pair * inner_width)
    grad_gate_inner = jnp.dot(normed.T, d_joined, preferred_element_type=jnp.float32).reshape(gate_inner.shape)
    grad_step = jnp.dot(normed.T, d_step_low, preferred_element_type=jnp.float32)
    grad_state = jnp.dot(normed.T, d_state_low, preferred_element_type=jnp.float32)
    d_normed = jnp.dot(d_joined, joined_weight.T, preferred_element_type=jnp.float32) + jnp.dot(d_step_low, step_weight.T, preferred_element_type=jnp.float32) + jnp.dot(d_state_low, state_weight.T, preferred_element_type=jnp.float32)
    grad_norm_gain = lax.optimization_barrier(jnp.sum(d_normed * stream * inv_rms, axis=0))
    scaled_rows = d_normed * norm_gain.astype(jnp.float32)[None, :]
    grad_in = gradient + inv_rms * scaled_rows - stream * inv_rms ** 3 * lax.optimization_barrier(jnp.sum(scaled_rows * stream, axis=1, keepdims=True)) / stream.shape[1]
    weight_grads = (grad_gate_inner, grad_step, grad_state, grad_conv_inner, grad_conv_inner_bias, grad_conv_state, grad_conv_state_bias, grad_norm_gain, grad_gate_gain, grad_out)
    return (grad_in, weight_grads, (grad_step_bias, grad_log_rate, grad_skip))

def run_full(stream_in, cotan_in, segment_ids, live_rows, stacked, head_params):
    same_seq, conv_masks = seq_structure(segment_ids)
    stream = jnp.where(live_rows, stream_in.astype(jnp.float32), 0.0)
    saved_layers = []
    for layer_num in range(LAYERS):
        gathered = tuple((weight_arr[layer_num] for weight_arr in stacked))
        head_vals = tuple((head_param[layer_num].astype(jnp.float32) for head_param in head_params))
        stream, kept_acts = forward_layer(stream, gathered, head_vals, same_seq, conv_masks)
        saved_layers.append((gathered, head_vals, kept_acts))
    gradient = jnp.where(live_rows, cotan_in.astype(jnp.float32), 0.0)
    collected = []
    for layer_num in reversed(range(LAYERS)):
        gathered, head_vals, kept_acts = saved_layers[layer_num]
        gradient, layer_grad, head_grad = backward_layer(gradient, gathered, head_vals, kept_acts, same_seq, conv_masks)
        collected.append(layer_grad + head_grad)
    collected = collected[::-1]
    stacked_grads = tuple((jnp.stack([layer_entry[slot_index] for layer_entry in collected]) for slot_index in range(13)))
    return (stream, gradient, stacked_grads)

def reference(block_input, cotangent, seq_len, norm_gain, gate_inner_proj, step_proj, state_proj, conv_inner, conv_inner_bias, conv_state, conv_state_bias, step_bias, log_rate, skip_gain, gate_gain, out_proj):
    half_axis = N_DP // 2
    home_input = block_input.reshape(N_DP, ROWS_IN, D)
    home_cot = cotangent.reshape(N_DP, ROWS_IN, D)
    home_len = seq_len.reshape(N_DP, SPD)
    stacked = (gate_inner_proj, step_proj, state_proj, conv_inner, conv_inner_bias, conv_state, conv_state_bias, norm_gain, gate_gain, out_proj)
    head_params = (step_bias, log_rate, skip_gain)
    zero_grads = tuple((jnp.zeros(weight_arr.shape, jnp.float32) for weight_arr in stacked + head_params))

    def pair_step(totals, pair_index):
        device_ids = (pair_index, pair_index + half_axis)
        input_pair = [lax.dynamic_index_in_dim(home_input, device_id, 0, keepdims=False) for device_id in device_ids]
        cot_pair = [lax.dynamic_index_in_dim(home_cot, device_id, 0, keepdims=False) for device_id in device_ids]
        len_pair = [lax.dynamic_index_in_dim(home_len, device_id, 0, keepdims=False) for device_id in device_ids]
        layouts = [balanced_layout(len_pair[0], len_pair[1]), balanced_layout(len_pair[1], len_pair[0])]
        outs_low = []
        grads_low = []
        for side_index in (0, 1):
            other_side = 1 - side_index
            segment_ids, live_rows, kept_rows = layouts[side_index]
            kept_other = layouts[other_side][2]
            stream_in = place_rows(input_pair[side_index], take_rows(input_pair[other_side], kept_other, LMAX), kept_rows, BAL)
            cotan_in = place_rows(cot_pair[side_index], take_rows(cot_pair[other_side], kept_other, LMAX), kept_rows, BAL)
            result, gradient, all_grads = run_full(stream_in, cotan_in, segment_ids, live_rows, stacked, head_params)
            totals = tuple((total_arr + grad_arr for total_arr, grad_arr in zip(totals, all_grads)))
            outs_low.append(result.astype(jnp.bfloat16))
            grads_low.append(gradient.astype(jnp.bfloat16))
        home_out = []
        home_grad = []
        for side_index in (0, 1):
            other_side = 1 - side_index
            kept_rows = layouts[side_index][2]
            kept_other = layouts[other_side][2]
            own_total = jnp.sum(len_pair[side_index]).astype(jnp.int32)
            live_home = (jnp.arange(ROWS_IN, dtype=jnp.int32) < own_total)[:, None]
            out_rows = place_rows(outs_low[side_index], take_rows(outs_low[other_side], kept_other, LMAX), kept_rows, ROWS_IN)
            grad_rows = place_rows(grads_low[side_index], take_rows(grads_low[other_side], kept_other, LMAX), kept_rows, ROWS_IN)
            zero_rows = jnp.zeros_like(out_rows)
            home_out.append(jnp.where(live_home, out_rows, zero_rows))
            home_grad.append(jnp.where(live_home, grad_rows, zero_rows))
        return (totals, (jnp.stack(home_out), jnp.stack(home_grad)))
    totals, (outs, grads) = lax.scan(pair_step, zero_grads, jnp.arange(half_axis, dtype=jnp.int32))
    block_out = jnp.transpose(outs, (1, 0, 2, 3)).reshape(N_DP * ROWS_IN, D)
    grad_input = jnp.transpose(grads, (1, 0, 2, 3)).reshape(N_DP * ROWS_IN, D)
    return (block_out, grad_input, totals[7], totals[0], totals[1], totals[2], totals[3], totals[4], totals[5], totals[6], totals[10], totals[11], totals[12], totals[8], totals[9])
```

```python
import functools

import jax
import jax.numpy as jnp
from jax import lax
from jax.experimental import pallas as pl
from jax.experimental.pallas import tpu as pltpu
from jax.sharding import PartitionSpec as P

E = 2048
KERNEL = 4
LAYERS = 2
LMAX = 64
BAL = 128
SMALL = 128


EPSILON = 1e-05
HIGHEST = lax.Precision.HIGHEST
HIGH = lax.Precision.HIGH


def swapped(array, axis, stride):
    return lax.ppermute(array, axis, [(i, i ^ 1 << stride) for i in range(lax.axis_size(axis))])


MESH = pl.DeviceIdType.MESH


def ring_chip(position, chips):
    half = chips // 2
    position = lax.rem(position + 2 * chips, chips)
    column = position // half
    level = position * (1 - column) + (chips - 1 - position) * column
    return level * 2 + column


def ring_place(chips):
    me = lax.axis_index("dp")
    core = lax.rem(me, 2)
    chip = me // 2
    column = lax.rem(chip, 2)
    level = chip // 2
    position = level * (1 - column) + (chips - 1 - level) * column
    return me, core, position


def remote(src, dst, send_sem, recv_sem, target):
    return pltpu.make_async_remote_copy(
        src_ref=src,
        dst_ref=dst,
        send_sem=send_sem,
        recv_sem=recv_sem,
        device_id={"dp": target},
        device_id_type=MESH,
    )


def gather_kernel(
    n,
    in_shard,
    out_shard,
    in_low,
    in_high,
    out_low,
    out_high,
    ring_send,
    ring_recv,
    core_send,
    core_recv,
    local_sem,
):
    chips = n // 2
    reach = chips // 2
    me, core, position = ring_place(chips)
    partner = me + 1 - 2 * core
    shards = (in_shard.at[0], out_shard.at[0], in_shard.at[1], out_shard.at[1])
    wholes = (in_low, out_low, in_high, out_high)

    def device_at(place):
        return ring_chip(place, chips) * 2 + core

    sides = (device_at(position + 1), device_at(position - 1))
    barrier = pltpu.get_barrier_semaphore()
    for target in (*sides, partner):
        pl.semaphore_signal(barrier, inc=1, device_id={"dp": target}, device_id_type=MESH)
    pl.semaphore_wait(barrier, 3)

    def pieces(step, flow):
        return (2 * flow, 2 * flow + 1) if step == reach else (0, 1, 2, 3)

    def ring_copy(source, slot, step, flow, piece):
        return remote(
            source,
            wholes[piece].at[slot],
            ring_send.at[flow, step - 1, piece],
            ring_recv.at[flow, step - 1, piece],
            sides[flow],
        )

    def core_copy(source, slot, index, piece):
        return remote(
            source,
            wholes[piece].at[slot],
            core_send.at[index, piece],
            core_recv.at[index, piece],
            partner,
        )

    sends = []
    for flow in range(2):
        for piece in pieces(1, flow):
            sends.append(ring_copy(shards[piece], me, 1, flow, piece))
            sends[-1].start()
    locals_ = []
    for piece in range(4):
        sends.append(core_copy(shards[piece], me, 0, piece))
        sends[-1].start()
        locals_.append(
            pltpu.make_async_copy(shards[piece], wholes[piece].at[me], local_sem.at[piece])
        )
        locals_[-1].start()
    for step in range(1, reach + 1):
        for flow in range(2):
            slot = device_at(position + (2 * flow - 1) * step)
            for piece in pieces(step, flow):
                arrived = wholes[piece].at[slot]
                ring_copy(arrived, slot, step, flow, piece).wait_recv()
                if step < reach and piece in pieces(step + 1, flow):
                    sends.append(ring_copy(arrived, slot, step + 1, flow, piece))
                    sends[-1].start()
                sends.append(core_copy(arrived, slot, 1 + flow * reach + step - 1, piece))
                sends[-1].start()
    other = me + 1 - 2 * core
    for piece in range(4):
        core_copy(wholes[piece].at[other], other, 0, piece).wait_recv()
    for step in range(1, reach + 1):
        for flow in range(2):
            slot = ring_chip(position + (2 * flow - 1) * step, chips) * 2 + 1 - core
            for piece in pieces(step, flow):
                core_copy(
                    wholes[piece].at[slot], slot, 1 + flow * reach + step - 1, piece
                ).wait_recv()
    for copy in sends:
        copy.wait_send()
    for copy in locals_:
        copy.wait()


def gather_weights(in_shard, out_shard, n):
    rows = in_shard.shape[1]
    reach = n // 4
    shapes = [
        jax.ShapeDtypeStruct((n, rows, shard.shape[2]), shard.dtype)
        for shard in (in_shard, in_shard, out_shard, out_shard)
    ]
    in_low, in_high, out_low, out_high = pl.pallas_call(
        functools.partial(gather_kernel, n),
        out_shape=shapes,
        in_specs=[pl.BlockSpec(memory_space=pltpu.VMEM)] * 2,
        out_specs=[pl.BlockSpec(memory_space=pl.ANY)] * 4,
        scratch_shapes=[
            pltpu.SemaphoreType.DMA((2, reach, 4)),
            pltpu.SemaphoreType.DMA((2, reach, 4)),
            pltpu.SemaphoreType.DMA((2 * reach + 1, 4)),
            pltpu.SemaphoreType.DMA((2 * reach + 1, 4)),
            pltpu.SemaphoreType.DMA((4,)),
        ],
        compiler_params=pltpu.CompilerParams(collective_id=0, has_side_effects=True),
        name="gather_weights",
    )(in_shard, out_shard)
    return tuple(
        (whole_in.reshape(n * rows, -1), whole_out.reshape(n * rows, -1))
        for whole_in, whole_out in ((in_low, out_low), (in_high, out_high))
    )


def scatter_kernel(
    n,
    parts,
    up_in,
    up_out,
    up_small,
    down_in,
    down_out,
    down_small,
    head_ref,
    out_ref,
    heads_ref,
    core_up,
    core_down,
    send_buf,
    recv_buf,
    core_send,
    core_recv,
    ring_send,
    ring_recv,
    head_send,
    head_recv,
):
    chips = n // 2
    me, core, position = ring_place(chips)
    partner = me + 1 - 2 * core
    grads = ((up_in, up_out, up_small), (down_in, down_out, down_small))
    cores = (core_up, core_down)

    def device_at(place):
        return ring_chip(place, chips) * 2 + core

    sides = (device_at(position + 1), device_at(position - 1))
    barrier = pltpu.get_barrier_semaphore()

    @pl.loop(1, n)
    def _(k):
        pl.semaphore_signal(
            barrier, inc=1, device_id={"dp": lax.rem(me + k, n)}, device_id_type=MESH
        )

    pl.semaphore_wait(barrier, n - 1)

    def shard_at(flow, step):
        return ring_chip(position + (2 * flow - 1) * step, chips)

    core_copies = {}
    for step in range(1, chips + 1):
        for flow in range(2):
            chip = shard_at(flow, step)
            for part, (array, start, place, size) in enumerate(parts):
                copy = remote(
                    grads[flow][array].at[2 * chip + 1 - core, :, pl.ds(start, size)],
                    cores[flow].at[step - 1, :, pl.ds(place, size)],
                    core_send.at[flow, step - 1, part],
                    core_recv.at[flow, step - 1, part],
                    partner,
                )
                copy.start()
                core_copies[flow, step, part] = copy

    @pl.loop(1, n)
    def _(k):
        remote(
            head_ref,
            heads_ref.at[me],
            head_send.at[k],
            head_recv.at[k],
            lax.rem(me + k, n),
        ).start()

    heads_ref[pl.ds(me, 1)] = head_ref[...][None]

    ring_copies = {}
    for step in range(1, chips + 1):
        for part, (array, start, place, size) in enumerate(parts):
            columns = pl.ds(place, size)
            for flow in range(2):
                own = 2 * shard_at(flow, step) + core
                core_copies[flow, step, part].wait_recv()
                total = grads[flow][array][own, :, pl.ds(start, size)].astype(
                    jnp.float32
                ) + cores[flow][step - 1, :, columns].astype(jnp.float32)
                if step > 1:
                    ring_copies[flow, step - 1, part].wait_recv()
                    total = total + recv_buf[flow, step - 2, :, columns].astype(jnp.float32)
                if step == chips:
                    out_ref[flow, :, columns] = total
                else:
                    send_buf[flow, step - 1, :, columns] = total.astype(jnp.bfloat16)
                    copy = remote(
                        send_buf.at[flow, step - 1, :, columns],
                        recv_buf.at[flow, step - 1, :, columns],
                        ring_send.at[flow, step - 1, part],
                        ring_recv.at[flow, step - 1, part],
                        sides[flow],
                    )
                    copy.start()
                    ring_copies[flow, step, part] = copy
    for copy in core_copies.values():
        copy.wait_send()
    for copy in ring_copies.values():
        copy.wait_send()

    @pl.loop(1, n)
    def _(k):
        sender = lax.rem(me - k + n, n)
        copy = remote(
            head_ref,
            heads_ref.at[sender],
            head_send.at[k],
            head_recv.at[k],
            lax.rem(me + k, n),
        )
        copy.wait_send()
        copy.wait_recv()


def scatter_grads(up, down, heads, widths, n):
    rows = up[0].shape[1]
    in_width = 2 * widths[0] + widths[1]
    out_width = up[1].shape[2]
    chips = n // 2
    cut = in_width // 256 * 128
    parts = (
        (0, 0, 0, cut),
        (0, cut, cut, in_width - cut),
        (1, 0, in_width, out_width),
        (2, 0, in_width + out_width, SMALL),
    )
    width = in_width + out_width + SMALL
    vmem = pl.BlockSpec(memory_space=pltpu.VMEM)
    return pl.pallas_call(
        functools.partial(scatter_kernel, n, parts),
        out_shape=(
            jax.ShapeDtypeStruct((2, rows, width), jnp.float32),
            jax.ShapeDtypeStruct((n,) + heads.shape, jnp.float32),
        ),
        in_specs=[vmem] * 7,
        out_specs=(vmem, vmem),
        scratch_shapes=[
            pltpu.VMEM((chips, rows, width), jnp.bfloat16),
            pltpu.VMEM((chips, rows, width), jnp.bfloat16),
            pltpu.VMEM((2, chips - 1, rows, width), jnp.bfloat16),
            pltpu.VMEM((2, chips - 1, rows, width), jnp.bfloat16),
            pltpu.SemaphoreType.DMA((2, chips, 4)),
            pltpu.SemaphoreType.DMA((2, chips, 4)),
            pltpu.SemaphoreType.DMA((2, chips - 1, 4)),
            pltpu.SemaphoreType.DMA((2, chips - 1, 4)),
            pltpu.SemaphoreType.DMA((n,)),
            pltpu.SemaphoreType.DMA((n,)),
        ],
        compiler_params=pltpu.CompilerParams(
            collective_id=1, has_side_effects=True, vmem_limit_bytes=60 * 1024 * 1024
        ),
        name="scatter_grads",
    )(*up, *down, heads)


def pair_sum(partial):
    low = partial.astype(jnp.bfloat16)
    other = swapped(low, "tensor", 0)
    return low.astype(jnp.float32) + other.astype(jnp.float32)


def pair_sum_wide(partial):
    return partial + swapped(partial, "tensor", 0)


def shifted(values, lag_rows):
    padding = jnp.zeros((lag_rows,) + values.shape[1:], values.dtype)
    return jnp.concatenate([padding, values[:-lag_rows]], axis=0)


def unshifted(values, lag_rows):
    padding = jnp.zeros((lag_rows,) + values.shape[1:], values.dtype)
    return jnp.concatenate([values[lag_rows:], padding], axis=0)


def silu_slope(values):
    sigmoid_val = jax.nn.sigmoid(values)
    return sigmoid_val * (1.0 + values * (1.0 - sigmoid_val))


def running_sum(lengths):
    index = jnp.arange(lengths.shape[0], dtype=jnp.int32)
    return jnp.sum(jnp.where(index[:, None] >= index[None, :], lengths[None, :], 0), axis=1)


def segments_of(lengths, row_total):
    ends = running_sum(lengths)
    position = jnp.arange(row_total, dtype=jnp.int32)
    return jnp.sum((position[:, None] >= ends[None, :]).astype(jnp.int32), axis=1)


def seq_structure(segment_ids):
    row_total = segment_ids.shape[0]
    position = jnp.arange(row_total, dtype=jnp.int32)
    same_seq = (
        (segment_ids[:, None] == segment_ids[None, :]) & (position[:, None] >= position[None, :])
    ).astype(jnp.float32)
    conv_masks = [None]
    for lag_rows in range(1, KERNEL):
        earlier = jnp.concatenate([jnp.full((lag_rows,), -1, jnp.int32), segment_ids[:-lag_rows]])
        conv_masks.append((segment_ids == earlier).astype(jnp.float32)[:, None])
    return (same_seq, conv_masks)


def conv_apply(source, kernel, bias_vec, conv_masks):
    tap_count = kernel.shape[0]
    result = bias_vec[None, :] + kernel[tap_count - 1][None, :] * source
    for lag_rows in range(1, tap_count):
        result = (
            result
            + kernel[tap_count - 1 - lag_rows][None, :]
            * shifted(source, lag_rows)
            * conv_masks[lag_rows]
        )
    return result


def conv_back(grad_pre, source, kernel, conv_masks):
    tap_count = kernel.shape[0]
    tap_grads = []
    grad_source = kernel[tap_count - 1][None, :] * grad_pre
    for tap_index in range(tap_count):
        lag_rows = tap_count - 1 - tap_index
        if lag_rows == 0:
            tap_grads.append(jnp.sum(grad_pre * source, axis=0))
        else:
            masked = grad_pre * conv_masks[lag_rows]
            tap_grads.append(jnp.sum(masked * shifted(source, lag_rows), axis=0))
            grad_source = grad_source + kernel[tap_index][None, :] * unshifted(masked, lag_rows)
    return (jnp.stack(tap_grads), jnp.sum(grad_pre, axis=0), grad_source)


def decay_matrix(cum_decay, same_seq):
    diff = cum_decay.T[:, :, None] - cum_decay.T[:, None, :]
    inside = same_seq[None, :, :] > 0.5
    return jnp.where(inside, jnp.exp(jnp.where(inside, diff, 0.0)), 0.0)


def take_rows(buffer, start_row, row_count):
    padding = jnp.zeros((row_count, buffer.shape[1]), buffer.dtype)
    return lax.dynamic_slice_in_dim(
        jnp.concatenate([buffer, padding], axis=0), start_row, row_count, 0
    )


def place_rows(own_rows, arrived, kept_rows, rows_out):
    row_width = own_rows.shape[1]
    if own_rows.shape[0] >= rows_out:
        base_rows = own_rows[:rows_out]
    else:
        base_rows = jnp.concatenate(
            [own_rows, jnp.zeros((rows_out - own_rows.shape[0], row_width), own_rows.dtype)], axis=0
        )
    extended = jnp.concatenate(
        [
            jnp.zeros((rows_out, row_width), own_rows.dtype),
            arrived,
            jnp.zeros((rows_out - arrived.shape[0], row_width), own_rows.dtype),
        ],
        axis=0,
    )
    moved_rows = lax.dynamic_slice_in_dim(extended, rows_out - kept_rows, rows_out, 0)
    position = jnp.arange(rows_out, dtype=jnp.int32)
    return jnp.where((position < kept_rows)[:, None], base_rows, moved_rows)


def balanced_layout(own_len, partner_len):
    own_end = running_sum(own_len)
    keep_flag = (own_end <= BAL).astype(jnp.int32)
    kept_rows = jnp.sum(own_len * keep_flag)
    partner_end = running_sum(partner_len)
    incoming = partner_len * (partner_end > BAL).astype(jnp.int32)
    segment_ids = segments_of(jnp.concatenate([own_len * keep_flag, incoming]), BAL)
    live_rows = (jnp.arange(BAL, dtype=jnp.int32) < kept_rows + jnp.sum(incoming))[:, None]
    return (segment_ids, live_rows, kept_rows)


def forward_layer(stream, gathered, head_vals, same_seq, conv_masks):
    (
        in_weight,
        conv_inner,
        conv_inner_bias,
        conv_state,
        conv_state_bias,
        norm_gain,
        gate_gain,
        out_weight,
        widths,
    ) = gathered
    inner_width, state_width, head_count = widths
    step_bias, log_rate, skip_gain = head_vals
    inv_rms = lax.rsqrt(jnp.mean(stream * stream, axis=1, keepdims=True) + EPSILON)
    normed = (stream * inv_rms * norm_gain.astype(jnp.float32)[None, :]).astype(jnp.bfloat16)
    joined = jnp.dot(normed, in_weight, preferred_element_type=jnp.float32)
    gate_pre = joined[:, :inner_width]
    inner_raw = joined[:, inner_width : 2 * inner_width]
    state_raw = joined[:, 2 * inner_width : 2 * inner_width + state_width]
    step_raw = joined[
        :, 2 * inner_width + state_width : 2 * inner_width + state_width + head_count
    ]
    inner_pre = conv_apply(
        inner_raw, conv_inner.astype(jnp.float32), conv_inner_bias.astype(jnp.float32), conv_masks
    )
    state_pre = conv_apply(
        state_raw, conv_state.astype(jnp.float32), conv_state_bias.astype(jnp.float32), conv_masks
    )
    inner_act = jax.nn.silu(inner_pre)
    state_act = jax.nn.silu(state_pre)
    half_state = state_act.shape[1] // 2
    state_in = state_act[:, :half_state]
    state_out = state_act[:, half_state:]
    step_size = jax.nn.softplus(step_raw + step_bias[None, :])
    decay_rate = -jnp.exp(log_rate)
    cum_decay = jnp.dot(same_seq, step_size * decay_rate[None, :], precision=HIGHEST)
    decay_mat = decay_matrix(cum_decay, same_seq)
    intersection = jnp.dot(state_out, state_in.T, precision=HIGH)
    total_rows, head_count = step_size.shape
    inner_heads = inner_act.reshape(total_rows, head_count, -1)
    scaled_in = inner_heads * step_size[:, :, None]
    mixer_mat = decay_mat * intersection[None]
    ssm_heads = (
        jnp.einsum("hts,shp->thp", mixer_mat, scaled_in, precision=HIGH)
        + skip_gain[None, :, None] * inner_heads
    )
    ssm_out = ssm_heads.reshape(total_rows, -1)
    gate_sig = jax.nn.sigmoid(gate_pre)
    gated_out = ssm_out * gate_pre * gate_sig
    square_sum = pair_sum_wide(jnp.sum(gated_out * gated_out, axis=1))
    inv_gate = lax.rsqrt(square_sum / E + EPSILON)[:, None]
    gate_normed = (gated_out * inv_gate * gate_gain.astype(jnp.float32)[None, :]).astype(
        jnp.bfloat16
    )
    partial_out = lax.dot_general(
        gate_normed, out_weight, (((1,), (1,)), ((), ())), preferred_element_type=jnp.float32
    )
    mixed = pair_sum(partial_out)
    kept_acts = (
        stream,
        inv_rms,
        normed,
        gate_pre,
        gate_sig,
        inner_raw,
        inner_pre,
        state_raw,
        state_pre,
        state_in,
        state_out,
        step_raw,
        step_size,
        decay_rate,
        decay_mat,
        intersection,
        inner_heads,
        scaled_in,
        ssm_out,
        gated_out,
        inv_gate,
        gate_normed,
    )
    return (stream + mixed, kept_acts)


def backward_layer(gradient, gathered, head_vals, kept_acts, same_seq, conv_masks):
    (
        in_weight,
        conv_inner,
        conv_inner_bias,
        conv_state,
        conv_state_bias,
        norm_gain,
        gate_gain,
        out_weight,
        widths,
    ) = gathered
    step_bias, log_rate, skip_gain = head_vals
    (
        stream,
        inv_rms,
        normed,
        gate_pre,
        gate_sig,
        inner_raw,
        inner_pre,
        state_raw,
        state_pre,
        state_in,
        state_out,
        step_raw,
        step_size,
        decay_rate,
        decay_mat,
        intersection,
        inner_heads,
        scaled_in,
        ssm_out,
        gated_out,
        inv_gate,
        gate_normed,
    ) = kept_acts
    grad_low = gradient.astype(jnp.bfloat16)
    grad_out = lax.dot_general(
        grad_low, gate_normed, (((0,), (0,)), ((), ())), preferred_element_type=jnp.float32
    ).astype(jnp.bfloat16)
    d_gate_normed = jnp.dot(grad_low, out_weight, preferred_element_type=jnp.float32)
    grad_gate_gain = jnp.sum(d_gate_normed * gated_out * inv_gate, axis=0)
    scaled_grad = d_gate_normed * gate_gain.astype(jnp.float32)[None, :]
    inner_sum = pair_sum_wide(jnp.sum(scaled_grad * gated_out, axis=1))[:, None]
    d_gated = inv_gate * scaled_grad - gated_out * inv_gate**3 * inner_sum / E
    d_ssm = d_gated * gate_pre * gate_sig
    d_gate_pre = d_gated * ssm_out * gate_sig * (1.0 + gate_pre * (1.0 - gate_sig))
    d_heads = d_ssm.reshape(inner_heads.shape)
    grad_skip = jnp.sum(d_heads * inner_heads, axis=(0, 2))
    mixer_mat = decay_mat * intersection[None]
    d_scaled = jnp.einsum("hts,thp->shp", mixer_mat, d_heads, precision=HIGH)
    d_mixer = jnp.einsum("thp,shp->hts", d_heads, scaled_in, precision=HIGH)
    d_intersection = jnp.sum(d_mixer * decay_mat, axis=0)
    flow_mat = d_mixer * mixer_mat
    d_cum = (jnp.sum(flow_mat, axis=2) - jnp.sum(flow_mat, axis=1)).T
    d_log_decay = jnp.dot(same_seq.T, d_cum, precision=HIGHEST)
    d_inner_heads = skip_gain[None, :, None] * d_heads + d_scaled * step_size[:, :, None]
    d_step = jnp.sum(d_scaled * inner_heads, axis=2) + d_log_decay * decay_rate[None, :]
    grad_log_rate = jnp.sum(d_log_decay * step_size, axis=0) * decay_rate
    d_state_out = jnp.dot(d_intersection, state_in, precision=HIGH)
    d_state_in = jnp.dot(d_intersection.T, state_out, precision=HIGH)
    d_step_raw = d_step * jax.nn.sigmoid(step_raw + step_bias[None, :])
    grad_step_bias = jnp.sum(d_step_raw, axis=0)
    d_state_act = pair_sum(jnp.concatenate([d_state_in, d_state_out], axis=1))
    d_inner_pre = d_inner_heads.reshape(inner_pre.shape) * silu_slope(inner_pre)
    d_state_pre = d_state_act * silu_slope(state_pre)
    grad_conv_inner, grad_conv_inner_bias, d_inner_raw = conv_back(
        d_inner_pre, inner_raw, conv_inner.astype(jnp.float32), conv_masks
    )
    grad_conv_state, grad_conv_state_bias, d_state_raw = conv_back(
        d_state_pre, state_raw, conv_state.astype(jnp.float32), conv_masks
    )
    d_joined = jnp.concatenate(
        [
            d_gate_pre,
            d_inner_raw,
            0.5 * d_state_raw,
            d_step_raw,
            jnp.zeros((d_step_raw.shape[0], SMALL - d_step_raw.shape[1]), jnp.float32),
        ],
        axis=1,
    ).astype(jnp.bfloat16)
    grad_in_weight = lax.dot_general(
        normed, d_joined, (((0,), (0,)), ((), ())), preferred_element_type=jnp.float32
    ).astype(jnp.bfloat16)
    grad_step = lax.dot_general(
        d_step_raw.astype(jnp.bfloat16),
        normed,
        (((0,), (0,)), ((), ())),
        preferred_element_type=jnp.float32,
    )
    partial_rows = lax.dot_general(
        d_joined, in_weight, (((1,), (1,)), ((), ())), preferred_element_type=jnp.float32
    )
    d_normed = pair_sum(partial_rows)
    grad_norm_gain = jnp.sum(d_normed * stream * inv_rms, axis=0)
    scaled_rows = d_normed * norm_gain.astype(jnp.float32)[None, :]
    grad_in = (
        gradient
        + inv_rms * scaled_rows
        - stream
        * inv_rms**3
        * jnp.sum(scaled_rows * stream, axis=1, keepdims=True)
        / stream.shape[1]
    )
    small_rows = (
        grad_step,
        grad_norm_gain,
        grad_conv_inner,
        grad_conv_inner_bias,
        grad_gate_gain,
        grad_conv_state,
        grad_conv_state_bias,
    )
    grads = pack_grads(grad_in_weight, grad_out, small_rows, widths)
    return (grad_in, grads, (grad_step_bias, grad_log_rate, grad_skip))


def pack_weights(stacked):
    (
        gate_inner_proj,
        step_proj,
        state_proj,
        conv_inner,
        conv_inner_bias,
        conv_state,
        conv_state_bias,
        norm_gain,
        gate_gain,
        out_proj,
    ) = stacked
    layers, rows = norm_gain.shape
    columns = [
        step_proj,
        norm_gain[:, :, None],
        jnp.swapaxes(conv_inner, 1, 2),
        conv_inner_bias[:, :, None],
        gate_gain[:, :, None],
        conv_state.reshape(layers, rows, 1),
        jnp.pad(conv_state_bias, ((0, 0), (0, rows - conv_state_bias.shape[1])))[:, :, None],
    ]
    used = sum(column.shape[2] for column in columns)
    columns.append(jnp.zeros((layers, rows, SMALL - used), norm_gain.dtype))
    in_shard = jnp.concatenate(
        [gate_inner_proj.reshape(layers, rows, -1), state_proj] + columns, axis=2
    )
    return in_shard, jnp.swapaxes(out_proj, 1, 2)


def unpack_weights(full, widths, n):
    inner_width, state_width, head_count = widths
    in_weight, out_weight = full
    small = in_weight[:, 2 * inner_width + state_width :].T[head_count : head_count + 9]
    per_device = state_width // n
    conv_state = (
        small[7].reshape(n, KERNEL, per_device).swapaxes(0, 1).reshape(KERNEL, state_width)
    )
    conv_state_bias = small[8].reshape(n, -1)[:, :per_device].reshape(state_width)
    return (
        in_weight,
        small[1:5],
        small[5],
        conv_state,
        conv_state_bias,
        small[0],
        small[6],
        out_weight,
        widths,
    )


def pack_grads(grad_in_weight, grad_out, small_rows, widths):
    step, norm_gain, conv_inner, conv_inner_bias, gate_gain, conv_state, conv_state_bias = (
        small_rows
    )
    inner_width, state_width, head_count = widths
    n = lax.axis_size("dp")
    per_device = state_width // n
    model = norm_gain.shape[0]
    state_flat = conv_state.reshape(KERNEL, n, per_device).swapaxes(0, 1).reshape(1, model)
    bias_flat = jnp.pad(
        conv_state_bias.reshape(n, per_device), ((0, 0), (0, model // n - per_device))
    ).reshape(1, model)
    small = jnp.concatenate(
        [
            step,
            norm_gain[None],
            conv_inner,
            conv_inner_bias[None],
            gate_gain[None],
            state_flat,
            bias_flat,
            jnp.zeros((SMALL - head_count - 9, model), jnp.float32),
        ]
    ).T.astype(jnp.bfloat16)
    return tuple(
        grad.reshape(n, model // n, -1) for grad in (grad_in_weight, grad_out, small)
    )


def unpack_grads(total, widths, n):
    inner_width, state_width, head_count = widths
    layers, rows = total.shape[:2]
    in_width = 2 * inner_width + state_width
    per_device = state_width // n
    small = total[:, :, total.shape[2] - SMALL :]
    step = small[:, :, :head_count]
    small = small[:, :, head_count : head_count + 9]
    return (
        total[:, :, : 2 * inner_width].reshape(layers, rows, 2, inner_width),
        step,
        2.0 * total[:, :, 2 * inner_width : in_width],
        jnp.swapaxes(small[:, :, 1:5], 1, 2),
        small[:, :, 5],
        small[:, :, 7].reshape(layers, KERNEL, per_device),
        small[:, :per_device, 8],
        small[:, :, 0],
        small[:, :, 6],
        jnp.swapaxes(total[:, :, in_width : total.shape[2] - SMALL], 1, 2),
    )


def run_blocks(stream_in, cotan_in, segment_ids, live_rows, stacked, head_params):
    same_seq, conv_masks = seq_structure(segment_ids)
    n = lax.axis_size("dp")
    widths = (stacked[0].shape[3], stacked[2].shape[2], stacked[1].shape[2])
    packed = gather_weights(*pack_weights(stacked), n)
    stream = jnp.where(live_rows, stream_in.astype(jnp.float32), 0.0)
    saved_layers = []
    for layer_num in range(LAYERS):
        gathered = unpack_weights(packed[layer_num], widths, n)
        head_vals = tuple((head_param[layer_num].astype(jnp.float32) for head_param in head_params))
        stream, kept_acts = forward_layer(stream, gathered, head_vals, same_seq, conv_masks)
        saved_layers.append((gathered, head_vals, kept_acts))
    gradient = jnp.where(live_rows, cotan_in.astype(jnp.float32), 0.0)
    layer_grads = [None] * LAYERS
    layer_heads = [None] * LAYERS
    for layer_num in reversed(range(LAYERS)):
        gathered, head_vals, kept_acts = saved_layers[layer_num]
        gradient, layer_grads[layer_num], layer_heads[layer_num] = backward_layer(
            gradient, gathered, head_vals, kept_acts, same_seq, conv_masks
        )
    head_block = jnp.stack([head for layer_entry in layer_heads for head in layer_entry])
    head_count = head_block.shape[1]
    head_rows = head_block.shape[0]
    head_block = jnp.pad(head_block, ((0, 8 - head_rows), (0, 128 - head_count)))
    total, head_parts = scatter_grads(layer_grads[0], layer_grads[1], head_block, widths, n)
    weight_grads = unpack_grads(total, widths, n)
    head_total = jnp.sum(head_parts, axis=0)[:head_rows, :head_count].reshape(
        LAYERS, 3, head_count
    )
    head_grads = tuple(head_total[:, slot_index] for slot_index in range(3))
    return (stream, gradient, weight_grads, head_grads)


def body(
    block_input,
    cotangent,
    seq_len,
    norm_gain,
    gate_inner_proj,
    step_proj,
    state_proj,
    conv_inner,
    conv_inner_bias,
    conv_state,
    conv_state_bias,
    step_bias,
    log_rate,
    skip_gain,
    gate_gain,
    out_proj,
):
    home_count = block_input.shape[0]
    own_total = jnp.sum(seq_len)
    live_home = (jnp.arange(home_count, dtype=jnp.int32) < own_total)[:, None]
    stacked = (
        gate_inner_proj,
        step_proj,
        state_proj,
        conv_inner,
        conv_inner_bias,
        conv_state,
        conv_state_bias,
        norm_gain,
        gate_gain,
        out_proj,
    )
    head_params = (step_bias, log_rate, skip_gain)
    partner_bit = lax.axis_size("dp").bit_length() - 2
    partner_len = swapped(seq_len, "dp", partner_bit)
    segment_ids, live_rows, kept_rows = balanced_layout(seq_len, partner_len)
    arrived = swapped(
        (take_rows(block_input, kept_rows, LMAX), take_rows(cotangent, kept_rows, LMAX)),
        "dp",
        partner_bit,
    )
    stream_in = place_rows(block_input, arrived[0], kept_rows, BAL)
    cotan_in = place_rows(cotangent, arrived[1], kept_rows, BAL)
    result, gradient, weight_grads, head_grads = run_blocks(
        stream_in, cotan_in, segment_ids, live_rows, stacked, head_params
    )
    out_rows = result.astype(jnp.bfloat16)
    grad_rows = gradient.astype(jnp.bfloat16)
    returned = swapped(
        (take_rows(out_rows, kept_rows, LMAX), take_rows(grad_rows, kept_rows, LMAX)),
        "dp",
        partner_bit,
    )
    out_rows = place_rows(out_rows, returned[0], kept_rows, home_count)
    grad_rows = place_rows(grad_rows, returned[1], kept_rows, home_count)
    zero_rows = jnp.zeros_like(out_rows)
    out_rows = jnp.where(live_home, out_rows, zero_rows)
    grad_rows = jnp.where(live_home, grad_rows, zero_rows)
    return (
        out_rows,
        grad_rows,
        weight_grads[7],
        weight_grads[0],
        weight_grads[1],
        weight_grads[2],
        weight_grads[3],
        weight_grads[4],
        weight_grads[5],
        weight_grads[6],
        head_grads[0],
        head_grads[1],
        head_grads[2],
        weight_grads[8],
        weight_grads[9],
    )


def solution(mesh):
    return jax.shard_map(
        body,
        mesh=mesh,
        in_specs=(
            P("dp", None),
            P("dp", None),
            P("dp"),
            P(None, "dp"),
            P(None, "dp", None, "tensor"),
            P(None, "dp", "tensor"),
            P(None, "dp", None),
            P(None, None, ("tensor", "dp")),
            P(None, ("tensor", "dp")),
            P(None, None, "dp"),
            P(None, "dp"),
            P(None, "tensor"),
            P(None, "tensor"),
            P(None, "tensor"),
            P(None, ("tensor", "dp")),
            P(None, "tensor", "dp"),
        ),
        out_specs=(
            P("dp", None),
            P("dp", None),
            P(None, "dp"),
            P(None, "dp", None, "tensor"),
            P(None, "dp", "tensor"),
            P(None, "dp", None),
            P(None, None, ("tensor", "dp")),
            P(None, ("tensor", "dp")),
            P(None, None, "dp"),
            P(None, "dp"),
            P(None, "tensor"),
            P(None, "tensor"),
            P(None, "tensor"),
            P(None, ("tensor", "dp")),
            P(None, "tensor", "dp"),
        ),
        check_vma=False,
    )
```

```python
import functools

import jax
import jax.numpy as jnp
from jax import lax
from jax.experimental import pallas as pl
from jax.experimental.pallas import tpu as pltpu
from jax.sharding import PartitionSpec as P

E = 2048
KERNEL = 4
LAYERS = 2
LMAX = 64
BAL = 128
SMALL = 128


EPSILON = 1e-05
HIGHEST = lax.Precision.HIGHEST


def swapped(array, axis, stride):
    return lax.ppermute(array, axis, [(i, i ^ 1 << stride) for i in range(lax.axis_size(axis))])


MESH = pl.DeviceIdType.MESH


def ring_chip(position, chips):
    half = chips // 2
    position = lax.rem(position + 2 * chips, chips)
    column = position // half
    level = position * (1 - column) + (chips - 1 - position) * column
    return level * 2 + column


def ring_place(chips):
    me = lax.axis_index("dp")
    core = lax.rem(me, 2)
    chip = me // 2
    column = lax.rem(chip, 2)
    level = chip // 2
    position = level * (1 - column) + (chips - 1 - level) * column
    return me, core, position


def remote(src, dst, send_sem, recv_sem, target):
    return pltpu.make_async_remote_copy(
        src_ref=src,
        dst_ref=dst,
        send_sem=send_sem,
        recv_sem=recv_sem,
        device_id={"dp": target},
        device_id_type=MESH,
    )


def gather_kernel(
    n,
    in_shard,
    out_shard,
    in_low,
    in_high,
    out_low,
    out_high,
    ring_send,
    ring_recv,
    core_send,
    core_recv,
    local_sem,
):
    chips = n // 2
    reach = chips // 2
    me, core, position = ring_place(chips)
    partner = me + 1 - 2 * core
    shards = (in_shard.at[0], out_shard.at[0], in_shard.at[1], out_shard.at[1])
    wholes = (in_low, out_low, in_high, out_high)

    def device_at(place):
        return ring_chip(place, chips) * 2 + core

    sides = (device_at(position + 1), device_at(position - 1))
    barrier = pltpu.get_barrier_semaphore()
    for target in (*sides, partner):
        pl.semaphore_signal(barrier, inc=1, device_id={"dp": target}, device_id_type=MESH)
    pl.semaphore_wait(barrier, 3)

    def pieces(step, flow):
        return (2 * flow, 2 * flow + 1) if step == reach else (0, 1, 2, 3)

    def ring_copy(source, slot, step, flow, piece):
        return remote(
            source,
            wholes[piece].at[slot],
            ring_send.at[flow, step - 1, piece],
            ring_recv.at[flow, step - 1, piece],
            sides[flow],
        )

    def core_copy(source, slot, index, piece):
        return remote(
            source,
            wholes[piece].at[slot],
            core_send.at[index, piece],
            core_recv.at[index, piece],
            partner,
        )

    sends = []
    for flow in range(2):
        for piece in pieces(1, flow):
            sends.append(ring_copy(shards[piece], me, 1, flow, piece))
            sends[-1].start()
    locals_ = []
    for piece in range(4):
        sends.append(core_copy(shards[piece], me, 0, piece))
        sends[-1].start()
        locals_.append(
            pltpu.make_async_copy(shards[piece], wholes[piece].at[me], local_sem.at[piece])
        )
        locals_[-1].start()
    for step in range(1, reach + 1):
        for flow in range(2):
            slot = device_at(position + (2 * flow - 1) * step)
            for piece in pieces(step, flow):
                arrived = wholes[piece].at[slot]
                ring_copy(arrived, slot, step, flow, piece).wait_recv()
                if step < reach and piece in pieces(step + 1, flow):
                    sends.append(ring_copy(arrived, slot, step + 1, flow, piece))
                    sends[-1].start()
                sends.append(core_copy(arrived, slot, 1 + flow * reach + step - 1, piece))
                sends[-1].start()
    other = me + 1 - 2 * core
    for piece in range(4):
        core_copy(wholes[piece].at[other], other, 0, piece).wait_recv()
    for step in range(1, reach + 1):
        for flow in range(2):
            slot = ring_chip(position + (2 * flow - 1) * step, chips) * 2 + 1 - core
            for piece in pieces(step, flow):
                core_copy(
                    wholes[piece].at[slot], slot, 1 + flow * reach + step - 1, piece
                ).wait_recv()
    for copy in sends:
        copy.wait_send()
    for copy in locals_:
        copy.wait()


def gather_weights(in_shard, out_shard, n):
    rows = in_shard.shape[1]
    reach = n // 4
    shapes = [
        jax.ShapeDtypeStruct((n, rows, shard.shape[2]), shard.dtype)
        for shard in (in_shard, in_shard, out_shard, out_shard)
    ]
    in_low, in_high, out_low, out_high = pl.pallas_call(
        functools.partial(gather_kernel, n),
        out_shape=shapes,
        in_specs=[pl.BlockSpec(memory_space=pltpu.VMEM)] * 2,
        out_specs=[pl.BlockSpec(memory_space=pl.ANY)] * 4,
        scratch_shapes=[
            pltpu.SemaphoreType.DMA((2, reach, 4)),
            pltpu.SemaphoreType.DMA((2, reach, 4)),
            pltpu.SemaphoreType.DMA((2 * reach + 1, 4)),
            pltpu.SemaphoreType.DMA((2 * reach + 1, 4)),
            pltpu.SemaphoreType.DMA((4,)),
        ],
        compiler_params=pltpu.CompilerParams(collective_id=0, has_side_effects=True),
        name="gather_weights",
    )(in_shard, out_shard)
    return tuple(
        (whole_in.reshape(n * rows, -1), whole_out.reshape(n * rows, -1))
        for whole_in, whole_out in ((in_low, out_low), (in_high, out_high))
    )


def scatter_kernel(
    n,
    parts,
    up_in,
    up_out,
    up_small,
    down_in,
    down_out,
    down_small,
    head_ref,
    out_ref,
    heads_ref,
    core_up,
    core_down,
    send_buf,
    recv_buf,
    core_send,
    core_recv,
    ring_send,
    ring_recv,
    head_send,
    head_recv,
):
    chips = n // 2
    me, core, position = ring_place(chips)
    partner = me + 1 - 2 * core
    grads = ((up_in, up_out, up_small), (down_in, down_out, down_small))
    cores = (core_up, core_down)

    def device_at(place):
        return ring_chip(place, chips) * 2 + core

    sides = (device_at(position + 1), device_at(position - 1))
    barrier = pltpu.get_barrier_semaphore()

    @pl.loop(1, n)
    def _(k):
        pl.semaphore_signal(
            barrier, inc=1, device_id={"dp": lax.rem(me + k, n)}, device_id_type=MESH
        )

    pl.semaphore_wait(barrier, n - 1)

    def shard_at(flow, step):
        return ring_chip(position + (2 * flow - 1) * step, chips)

    core_copies = {}
    for step in range(1, chips + 1):
        for flow in range(2):
            chip = shard_at(flow, step)
            for part, (array, start, place, size) in enumerate(parts):
                copy = remote(
                    grads[flow][array].at[2 * chip + 1 - core, :, pl.ds(start, size)],
                    cores[flow].at[step - 1, :, pl.ds(place, size)],
                    core_send.at[flow, step - 1, part],
                    core_recv.at[flow, step - 1, part],
                    partner,
                )
                copy.start()
                core_copies[flow, step, part] = copy

    @pl.loop(1, n)
    def _(k):
        remote(
            head_ref,
            heads_ref.at[me],
            head_send.at[k],
            head_recv.at[k],
            lax.rem(me + k, n),
        ).start()

    heads_ref[pl.ds(me, 1)] = head_ref[...][None]

    ring_copies = {}
    for step in range(1, chips + 1):
        for part, (array, start, place, size) in enumerate(parts):
            columns = pl.ds(place, size)
            for flow in range(2):
                own = 2 * shard_at(flow, step) + core
                core_copies[flow, step, part].wait_recv()
                total = grads[flow][array][own, :, pl.ds(start, size)].astype(
                    jnp.float32
                ) + cores[flow][step - 1, :, columns].astype(jnp.float32)
                if step > 1:
                    ring_copies[flow, step - 1, part].wait_recv()
                    total = total + recv_buf[flow, step - 2, :, columns].astype(jnp.float32)
                if step == chips:
                    out_ref[flow, :, columns] = total
                else:
                    send_buf[flow, step - 1, :, columns] = total.astype(jnp.bfloat16)
                    copy = remote(
                        send_buf.at[flow, step - 1, :, columns],
                        recv_buf.at[flow, step - 1, :, columns],
                        ring_send.at[flow, step - 1, part],
                        ring_recv.at[flow, step - 1, part],
                        sides[flow],
                    )
                    copy.start()
                    ring_copies[flow, step, part] = copy
    for copy in core_copies.values():
        copy.wait_send()
    for copy in ring_copies.values():
        copy.wait_send()

    @pl.loop(1, n)
    def _(k):
        sender = lax.rem(me - k + n, n)
        copy = remote(
            head_ref,
            heads_ref.at[sender],
            head_send.at[k],
            head_recv.at[k],
            lax.rem(me + k, n),
        )
        copy.wait_send()
        copy.wait_recv()


def scatter_grads(up, down, heads, widths, n):
    rows = up[0].shape[1]
    in_width = 2 * widths[0] + widths[1]
    out_width = up[1].shape[2]
    chips = n // 2
    cut = in_width // 256 * 128
    parts = (
        (0, 0, 0, cut),
        (0, cut, cut, in_width - cut),
        (1, 0, in_width, out_width),
        (2, 0, in_width + out_width, SMALL),
    )
    width = in_width + out_width + SMALL
    vmem = pl.BlockSpec(memory_space=pltpu.VMEM)
    return pl.pallas_call(
        functools.partial(scatter_kernel, n, parts),
        out_shape=(
            jax.ShapeDtypeStruct((2, rows, width), jnp.float32),
            jax.ShapeDtypeStruct((n,) + heads.shape, jnp.float32),
        ),
        in_specs=[vmem] * 7,
        out_specs=(vmem, vmem),
        scratch_shapes=[
            pltpu.VMEM((chips, rows, width), jnp.bfloat16),
            pltpu.VMEM((chips, rows, width), jnp.bfloat16),
            pltpu.VMEM((2, chips - 1, rows, width), jnp.bfloat16),
            pltpu.VMEM((2, chips - 1, rows, width), jnp.bfloat16),
            pltpu.SemaphoreType.DMA((2, chips, 4)),
            pltpu.SemaphoreType.DMA((2, chips, 4)),
            pltpu.SemaphoreType.DMA((2, chips - 1, 4)),
            pltpu.SemaphoreType.DMA((2, chips - 1, 4)),
            pltpu.SemaphoreType.DMA((n,)),
            pltpu.SemaphoreType.DMA((n,)),
        ],
        compiler_params=pltpu.CompilerParams(
            collective_id=1, has_side_effects=True, vmem_limit_bytes=60 * 1024 * 1024
        ),
        name="scatter_grads",
    )(*up, *down, heads)


F32 = jnp.float32
BF16 = jnp.bfloat16
VROWS = 16
NN = (((1,), (0,)), ((), ()))
NT = (((1,), (1,)), ((), ()))
TN = (((0,), (0,)), ((), ()))


def mul(a, b, dims=NN):
    return lax.dot_general(
        a.astype(BF16), b.astype(BF16), dims, preferred_element_type=F32
    )


def mul_wide(a, b, dims=NN):
    return lax.dot_general(a, b, dims, precision=HIGHEST, preferred_element_type=F32)


def mul_split(a, b, dims=NN):
    high = a.astype(BF16)
    low = (a - high.astype(F32)).astype(BF16)
    return mul(high, b, dims) + mul(low, b, dims)


def iota(shape, axis):
    return lax.broadcasted_iota(jnp.int32, shape, axis)


def one_hot(mask):
    return jnp.where(mask, 1.0, 0.0).astype(BF16)


def row_picker(head_count):
    shape = (VROWS, SMALL)
    return one_hot(iota(shape, 0) + head_count == iota(shape, 1))


def state_picker(model, state_width, n):
    per_device = state_width // n
    shape = (model, state_width)
    column = iota(shape, 1)
    owner = lax.shift_right_logical(column, per_device.bit_length() - 1)
    return one_hot(
        iota(shape, 0) == owner * (model // n) + jnp.bitwise_and(column, per_device - 1)
    )


def head_picker(inner_width, head_count):
    head_size = inner_width // head_count
    shape = (inner_width, SMALL)
    return one_hot(
        lax.shift_right_logical(iota(shape, 0), head_size.bit_length() - 1) == iota(shape, 1)
    )


def slope_of(values):
    sigmoid_val = jax.nn.sigmoid(values)
    return sigmoid_val * (1.0 + values * (1.0 - sigmoid_val))


def softplus(values):
    return jnp.maximum(values, 0.0) + jnp.log1p(jnp.exp(-jnp.abs(values)))


def causal_conv(raw, taps, bias, masks):
    total = bias + taps[KERNEL - 1 : KERNEL] * raw
    for lag in range(1, KERNEL):
        tap = KERNEL - 1 - lag
        total = total + taps[tap : tap + 1] * (pltpu.roll(raw, lag, 0) * masks[:, lag : lag + 1])
    return total


def causal_conv_back(grad, raw, taps, masks):
    rows = grad.shape[0]
    tap_grads = [None] * KERNEL
    tap_grads[KERNEL - 1] = jnp.sum(grad * raw, axis=0, keepdims=True)
    source = taps[KERNEL - 1 : KERNEL] * grad
    for lag in range(1, KERNEL):
        tap = KERNEL - 1 - lag
        masked = grad * masks[:, lag : lag + 1]
        tap_grads[tap] = jnp.sum(masked * pltpu.roll(raw, lag, 0), axis=0, keepdims=True)
        source = source + taps[tap : tap + 1] * pltpu.roll(masked, rows - lag, 0)
    return tap_grads + [jnp.sum(grad, axis=0, keepdims=True)], source


def row_scale(stream):
    return lax.rsqrt(jnp.mean(stream * stream, axis=1, keepdims=True) + EPSILON)


def pair_blocks(head_count, inner_width):
    head_size = inner_width // head_count
    per_block = SMALL // head_size
    return [
        (slice(block * SMALL, (block + 1) * SMALL), range(block * per_block, (block + 1) * per_block))
        for block in range(inner_width // SMALL)
    ]


def spread(columns, heads, head_size):
    rows = columns.shape[0]
    lane_head = lax.shift_right_logical(iota((rows, SMALL), 1), head_size.bit_length() - 1)
    total = columns[:, heads[0] : heads[0] + 1]
    for place in range(1, len(heads)):
        total = jnp.where(lane_head >= place, columns[:, heads[place] : heads[place] + 1], total)
    return jnp.broadcast_to(total, (rows, SMALL))


def head_lanes(rows, head_size, place):
    lane_head = lax.shift_right_logical(iota((rows, SMALL), 1), head_size.bit_length() - 1)
    return lane_head == place


def decay_of(cum, cum_t, head, inside):
    diff = cum[:, head : head + 1] - cum_t[head : head + 1, :]
    return jnp.exp(jnp.where(inside, diff, -1e30))


ACTS = (
    ("normed", BF16, "model"),
    ("gate_pre", F32, "inner"),
    ("inner_raw", F32, "inner"),
    ("inner_pre", F32, "inner"),
    ("ssm", F32, "inner"),
    ("state_raw", F32, "state"),
    ("state_pre", F32, "state"),
    ("step_raw", F32, "small"),
    ("cum", F32, "small"),
    ("vec", F32, "model"),
    ("vec_state", F32, "state"),
)


def act_shapes(model, widths):
    inner_width, state_width, _ = widths
    width_of = {"model": model, "inner": inner_width, "state": state_width, "small": SMALL}
    return [
        jax.ShapeDtypeStruct(
            (VROWS if name.startswith("vec") else BAL, width_of[kind]), dtype
        )
        for name, dtype, kind in ACTS
    ]


def named(refs):
    return dict(zip([name for name, _, _ in ACTS], refs))


def forward_part(stream, w_in, w_out, head_ref, same_ref, mask_ref, acts, widths, n):
    inner_width, state_width, head_count = widths
    model = stream.shape[1]
    rows = stream.shape[0]
    head_size = inner_width // head_count
    half = state_width // 2
    at_state = 2 * inner_width
    at_small = at_state + state_width
    masks = mask_ref[...]
    inside = same_ref[...] > 0.5
    vec = mul(row_picker(head_count), w_in[:, at_small : at_small + SMALL], NT)
    vec_state = mul(vec, state_picker(model, state_width, n))
    acts["vec"][...] = vec
    acts["vec_state"][...] = vec_state
    normed = (stream * row_scale(stream) * vec[0:1]).astype(BF16)
    acts["normed"][...] = normed
    state_step = mul(normed, w_in[:, at_state : at_small + SMALL])
    state_raw = state_step[:, :state_width]
    step_raw = state_step[:, state_width:] + head_ref[0:1]
    acts["state_raw"][...] = state_raw
    acts["step_raw"][...] = step_raw
    state_pre = causal_conv(state_raw, vec_state[7:11], vec_state[11:12], masks)
    acts["state_pre"][...] = state_pre
    state = state_pre * jax.nn.sigmoid(state_pre)
    step = softplus(step_raw)
    rate = -jnp.exp(head_ref[1:2])
    cum = mul_wide(same_ref[...], step * rate)
    acts["cum"][...] = cum
    cum_t = cum.T
    intersection = mul(state[:, half:], state[:, :half], NT)
    inner_raw = mul(normed, w_in[:, inner_width:at_state])
    acts["inner_raw"][...] = inner_raw
    inner_pre = causal_conv(inner_raw, vec[1:5], vec[5:6], masks)
    acts["inner_pre"][...] = inner_pre
    gate_pre = mul(normed, w_in[:, :inner_width])
    acts["gate_pre"][...] = gate_pre
    skip = head_ref[2:3]
    pieces = []
    square = jnp.zeros((rows, 1), F32)
    for lanes, heads in pair_blocks(head_count, inner_width):
        pre = inner_pre[:, lanes]
        inner = pre * jax.nn.sigmoid(pre)
        scaled = (inner * spread(step, heads, head_size)).astype(BF16)
        out = spread(skip, heads, head_size) * inner
        for place, head in enumerate(heads):
            mixer = decay_of(cum, cum_t, head, inside) * intersection
            out = out + jnp.where(head_lanes(rows, head_size, place), mul(mixer, scaled), 0.0)
        acts["ssm"][:, lanes] = out
        gate = gate_pre[:, lanes]
        gated = out * gate * jax.nn.sigmoid(gate)
        square = square + jnp.sum(gated * gated, axis=1, keepdims=True)
        pieces.append((gated * vec[6:7, lanes]).astype(BF16))
    partial = mul(jnp.concatenate(pieces, axis=1), w_out[...], NT)
    return partial.astype(BF16), jnp.broadcast_to(square, (rows, SMALL))


def mixed_of(part, other, square, other_square):
    total = part.astype(F32) + other.astype(F32)
    return total, lax.rsqrt((square + other_square)[:, 0:1] / E + EPSILON)


def backward_part(
    grad, total, inv_gate, w_in, w_out, head_ref, same_ref, mask_ref, acts, joined_ref, turn_ref,
    grad_in, grad_out, grad_small, vec_grads, widths, n, shard
):
    inner_width, state_width, head_count = widths
    rows, model = grad.shape
    head_size = inner_width // head_count
    half = state_width // 2
    at_state = 2 * inner_width
    at_small = at_state + state_width
    masks = mask_ref[...]
    inside = same_ref[...] > 0.5
    vec = acts["vec"][...]
    vec_state = acts["vec_state"][...]
    grad_low = grad.astype(BF16)
    inner_sum = jnp.sum(grad_low.astype(F32) * total, axis=1, keepdims=True)
    pull = inv_gate * inv_gate * inv_gate * inner_sum / E
    step_raw = acts["step_raw"][...]
    step = softplus(step_raw)
    rate = -jnp.exp(head_ref[1:2])
    skip = head_ref[2:3]
    cum = acts["cum"][...]
    cum_t = cum.T
    state_pre = acts["state_pre"][...]
    state = state_pre * jax.nn.sigmoid(state_pre)
    intersection = mul(state[:, half:], state[:, :half], NT)
    d_gate_normed = mul(grad_low, w_out[...])
    d_intersection = jnp.zeros((rows, rows), F32)
    row_part = jnp.zeros((rows, SMALL), F32)
    column_part = jnp.zeros((SMALL, rows), F32)
    head_lane = iota((rows, SMALL), 1)
    head_row = iota((SMALL, rows), 0)
    gain_grads = []
    skip_parts = []
    step_parts = []
    inner_taps = []
    gate_pieces = []
    for lanes, heads in pair_blocks(head_count, inner_width):
        pre = acts["inner_pre"][:, lanes]
        sigmoid_inner = jax.nn.sigmoid(pre)
        inner = pre * sigmoid_inner
        gate = acts["gate_pre"][:, lanes]
        gate_sig = jax.nn.sigmoid(gate)
        ssm = acts["ssm"][:, lanes]
        act = gate * gate_sig
        gated = ssm * act
        gain = vec[6:7, lanes]
        d_normed = d_gate_normed[:, lanes]
        gain_grads.append(jnp.sum(d_normed * gated * inv_gate, axis=0, keepdims=True))
        gate_pieces.append((gated * inv_gate * gain).astype(BF16))
        d_gated = inv_gate * gain * d_normed - gated * pull
        d_ssm = d_gated * act
        joined_ref[:, lanes] = (
            d_gated * ssm * gate_sig * (1.0 + gate * (1.0 - gate_sig))
        ).astype(BF16)
        skip_parts.append(jnp.sum(d_ssm * inner, axis=0, keepdims=True))
        step_wide = spread(step, heads, head_size)
        scaled = (inner * step_wide).astype(BF16)
        d_low = d_ssm.astype(BF16)
        d_scaled = jnp.zeros((rows, SMALL), F32)
        for place, head in enumerate(heads):
            mine = head_lanes(rows, head_size, place)
            decay = decay_of(cum, cum_t, head, inside)
            mixer = decay * intersection
            d_scaled = d_scaled + jnp.where(mine, mul(mixer, d_low, TN), 0.0)
            d_mixer = mul(jnp.where(mine, d_ssm, 0.0), scaled, NT)
            d_decayed = d_mixer * decay
            d_intersection = d_intersection + d_decayed
            flow = d_decayed * intersection
            row_part = jnp.where(
                head_lane == head, jnp.sum(flow, axis=1, keepdims=True), row_part
            )
            column_part = jnp.where(
                head_row == head, jnp.sum(flow, axis=0, keepdims=True), column_part
            )
        step_parts.append(d_scaled * inner)
        d_inner = spread(skip, heads, head_size) * d_ssm + d_scaled * step_wide
        d_pre = d_inner * (sigmoid_inner * (1.0 + pre * (1.0 - sigmoid_inner)))
        taps, d_raw = causal_conv_back(
            d_pre, acts["inner_raw"][:, lanes], vec[1:5, lanes], masks
        )
        inner_taps.append(taps)
        joined_ref[:, slice(inner_width + lanes.start, inner_width + lanes.stop)] = d_raw.astype(
            BF16
        )
    gate_normed = jnp.concatenate(gate_pieces, axis=1)
    d_log = mul_wide(same_ref[...], row_part - column_part.T, TN)
    picker = head_picker(inner_width, head_count)
    d_step = mul_split(jnp.concatenate(step_parts, axis=1), picker) + d_log * rate
    d_step_raw = jnp.where(head_lane < head_count, d_step * jax.nn.sigmoid(step_raw), 0.0)
    skip_row = jnp.broadcast_to(jnp.concatenate(skip_parts, axis=1), (8, inner_width))
    head_grads = (
        jnp.sum(d_step_raw, axis=0, keepdims=True),
        jnp.sum(d_log * step, axis=0, keepdims=True) * rate,
        mul_split(skip_row, picker)[0:1],
    )
    d_state = jnp.concatenate(
        [mul(d_intersection, state[:, half:], TN), mul(d_intersection, state[:, :half])], axis=1
    )
    state_taps, d_state_raw = causal_conv_back(
        d_state * slope_of(state_pre), acts["state_raw"][...], vec_state[7:11], masks
    )
    joined_ref[:, at_state:at_small] = d_state_raw.astype(BF16)
    joined_ref[:, at_small : at_small + SMALL] = d_step_raw.astype(BF16)
    partial = mul(joined_ref[...], w_in[...], NT).astype(BF16)
    state_rows = jnp.concatenate(
        [jnp.zeros((7, state_width), F32)]
        + state_taps
        + [jnp.zeros((VROWS - 12, state_width), F32)]
    )
    vec_grads[...] = mul(state_rows, state_picker(model, state_width, n), NT)
    vec_grads[1:7] = jnp.concatenate(
        [
            jnp.concatenate([taps[row] for taps in inner_taps], axis=1)
            for row in range(KERNEL + 1)
        ]
        + [jnp.concatenate(gain_grads, axis=1)]
    )

    def write_grads():
        turn_ref[...] = acts["normed"][...].astype(F32).T.astype(BF16)
        per = SMALL // shard
        for block in range(model // SMALL):
            mine = slice(block * SMALL, (block + 1) * SMALL)
            product = mul(turn_ref[mine], joined_ref[...])
            grad_in[block * per : (block + 1) * per] = product[:, :at_small].reshape(
                per, shard, at_small
            ).astype(BF16)
            grad_small[mine] = product[:, at_small:]
        turn_ref[...] = grad.T.astype(BF16)
        for block in range(model // SMALL):
            mine = slice(block * SMALL, (block + 1) * SMALL)
            grad_out[block * per : (block + 1) * per] = (
                mul(turn_ref[mine], gate_normed).reshape(per, shard, inner_width).astype(BF16)
            )

    return partial, head_grads, write_grads


def finish_part(d_normed, grad, stream, acts, vec_grads, grad_small, small_out, head_count, shard):
    model = stream.shape[1]
    inv_rms = row_scale(stream)
    vec_grads[0:1] = jnp.sum(d_normed * stream * inv_rms, axis=0, keepdims=True)
    small = grad_small[...] + mul(vec_grads[...], row_picker(head_count), TN)
    small_out[...] = small.reshape(model // shard, shard, SMALL).astype(BF16)
    scaled = d_normed * acts["vec"][0:1]
    return (
        grad
        + inv_rms * scaled
        - stream
        * (inv_rms * inv_rms * inv_rms)
        * jnp.sum(scaled * stream, axis=1, keepdims=True)
        / model
    )


def running_sum(lengths):
    index = jnp.arange(lengths.shape[0], dtype=jnp.int32)
    return jnp.sum(jnp.where(index[:, None] >= index[None, :], lengths[None, :], 0), axis=1)


def segments_of(lengths, row_total):
    ends = running_sum(lengths)
    position = jnp.arange(row_total, dtype=jnp.int32)
    return jnp.sum((position[:, None] >= ends[None, :]).astype(jnp.int32), axis=1)


def seq_structure(segment_ids):
    row_total = segment_ids.shape[0]
    position = jnp.arange(row_total, dtype=jnp.int32)
    same_seq = (
        (segment_ids[:, None] == segment_ids[None, :]) & (position[:, None] >= position[None, :])
    ).astype(jnp.float32)
    conv_masks = [None]
    for lag_rows in range(1, KERNEL):
        earlier = jnp.concatenate([jnp.full((lag_rows,), -1, jnp.int32), segment_ids[:-lag_rows]])
        conv_masks.append((segment_ids == earlier).astype(jnp.float32)[:, None])
    return (same_seq, conv_masks)


def take_rows(buffer, start_row, row_count):
    padding = jnp.zeros((row_count, buffer.shape[1]), buffer.dtype)
    return lax.dynamic_slice_in_dim(
        jnp.concatenate([buffer, padding], axis=0), start_row, row_count, 0
    )


def place_rows(own_rows, arrived, kept_rows, rows_out):
    row_width = own_rows.shape[1]
    if own_rows.shape[0] >= rows_out:
        base_rows = own_rows[:rows_out]
    else:
        base_rows = jnp.concatenate(
            [own_rows, jnp.zeros((rows_out - own_rows.shape[0], row_width), own_rows.dtype)], axis=0
        )
    extended = jnp.concatenate(
        [
            jnp.zeros((rows_out, row_width), own_rows.dtype),
            arrived,
            jnp.zeros((rows_out - arrived.shape[0], row_width), own_rows.dtype),
        ],
        axis=0,
    )
    moved_rows = lax.dynamic_slice_in_dim(extended, rows_out - kept_rows, rows_out, 0)
    position = jnp.arange(rows_out, dtype=jnp.int32)
    return jnp.where((position < kept_rows)[:, None], base_rows, moved_rows)


def balanced_layout(own_len, partner_len):
    own_end = running_sum(own_len)
    keep_flag = (own_end <= BAL).astype(jnp.int32)
    kept_rows = jnp.sum(own_len * keep_flag)
    partner_end = running_sum(partner_len)
    incoming = partner_len * (partner_end > BAL).astype(jnp.int32)
    segment_ids = segments_of(jnp.concatenate([own_len * keep_flag, incoming]), BAL)
    live_rows = (jnp.arange(BAL, dtype=jnp.int32) < kept_rows + jnp.sum(incoming))[:, None]
    return (segment_ids, live_rows, kept_rows)


def pad_rows(array, rows):
    return jnp.pad(array, ((0, 0), (0, rows - array.shape[1]), (0, 0)))


def pack_weights(stacked):
    (
        gate_inner_proj,
        step_proj,
        state_proj,
        conv_inner,
        conv_inner_bias,
        conv_state,
        conv_state_bias,
        norm_gain,
        gate_gain,
        out_proj,
    ) = stacked
    layers, rows = norm_gain.shape
    columns = [
        step_proj,
        norm_gain[:, :, None],
        jnp.swapaxes(conv_inner, 1, 2),
        conv_inner_bias[:, :, None],
        gate_gain[:, :, None],
        pad_rows(jnp.swapaxes(conv_state, 1, 2), rows),
        pad_rows(conv_state_bias[:, :, None], rows),
    ]
    used = sum(column.shape[2] for column in columns)
    columns.append(jnp.zeros((layers, rows, SMALL - used), norm_gain.dtype))
    in_shard = jnp.concatenate(
        [gate_inner_proj.reshape(layers, rows, -1), state_proj] + columns, axis=2
    )
    return in_shard, jnp.swapaxes(out_proj, 1, 2)


def unpack_grads(total, widths, n):
    inner_width, state_width, head_count = widths
    layers, rows = total.shape[:2]
    in_width = 2 * inner_width + state_width
    per_device = state_width // n
    small = total[:, :, total.shape[2] - SMALL :]
    step = small[:, :, :head_count]
    small = small[:, :, head_count : head_count + 12]
    shared = jnp.concatenate(
        [total[:, :, 2 * inner_width : in_width], jnp.pad(small[:, :, 7:12], ((0, 0), (0, 0), (0, SMALL - 5)))],
        axis=2,
    )
    shared = shared + swapped(shared, "tensor", 0)
    state = shared[:, :per_device, state_width:]
    return (
        total[:, :, : 2 * inner_width].reshape(layers, rows, 2, inner_width),
        step,
        shared[:, :, :state_width],
        jnp.swapaxes(small[:, :, 1:5], 1, 2),
        small[:, :, 5],
        jnp.swapaxes(state[:, :, :KERNEL], 1, 2),
        state[:, :, KERNEL],
        small[:, :, 0],
        small[:, :, 6],
        jnp.swapaxes(total[:, :, in_width : total.shape[2] - SMALL], 1, 2),
    )


def call(body, name, operands, outs, scratch=()):
    vmem = pl.BlockSpec(memory_space=pltpu.VMEM)
    return pl.pallas_call(
        body,
        out_shape=tuple(outs),
        in_specs=[vmem] * len(operands),
        out_specs=(vmem,) * len(outs),
        scratch_shapes=list(scratch),
        compiler_params=pltpu.CompilerParams(vmem_limit_bytes=56 * 1024 * 1024),
        name=name,
    )(*operands)


def shape(rows, columns, dtype):
    return jax.ShapeDtypeStruct((rows, columns), dtype)


def live_of(values, mask_ref):
    return jnp.where(mask_ref[:, KERNEL : KERNEL + 1] > 0.5, values[...].astype(F32), 0.0)


def first_forward(widths, n, rows_in, w_in, w_out, head, same, mask, stream, part, square, *acts):
    stream[...] = live_of(rows_in, mask)
    part[...], square[...] = forward_part(
        stream[...], w_in, w_out, head, same, mask, named(acts), widths, n
    )


def next_forward(
    widths, n, before, part_in, other_in, square_in, other_square, w_in, w_out, head, same, mask,
    stream, total, inv, part, square, *acts
):
    total[...], scale = mixed_of(part_in[...], other_in[...], square_in[...], other_square[...])
    inv[...] = jnp.broadcast_to(scale, inv.shape)
    stream[...] = before[...] + total[...] * scale
    part[...], square[...] = forward_part(
        stream[...], w_in, w_out, head, same, mask, named(acts), widths, n
    )


def write_heads(head_grads, heads):
    for row, grads in enumerate(head_grads):
        heads[row : row + 1] = grads
    heads[len(head_grads) :] = jnp.zeros((8 - len(head_grads), SMALL), F32)


def last_backward(
    widths, n, before, part_in, other_in, square_in, other_square, rows_in, w_in, w_out, head, same,
    mask, *rest
):
    acts, rest = named(rest[: len(ACTS)]), rest[len(ACTS) :]
    result, partial, grad_in, grad_out, grad_small, vec_grads, heads, joined, turn = rest
    total, scale = mixed_of(part_in[...], other_in[...], square_in[...], other_square[...])
    result[...] = (before[...] + total * scale).astype(BF16)
    partial[...], head_grads, write_grads = backward_part(
        live_of(rows_in, mask), total, scale, w_in, w_out, head, same, mask, acts, joined, turn,
        grad_in, grad_out, grad_small, vec_grads, widths, n, grad_in.shape[1]
    )
    write_grads()
    write_heads(head_grads, heads)


def next_backward(
    widths, n, part_in, other_in, rows_in, stream, late_vec, late_vec_grads, late_small, total, inv,
    w_in, w_out, head, same, mask, *rest
):
    acts, rest = named(rest[: len(ACTS)]), rest[len(ACTS) :]
    (
        small_out, grad_ref, partial, grad_in, grad_out, grad_small, vec_grads, heads, joined, turn,
        kept
    ) = rest
    kept[...] = late_vec_grads[...]
    grad_ref[...] = finish_part(
        part_in[...].astype(F32) + other_in[...].astype(F32), live_of(rows_in, mask), stream[...],
        {"vec": late_vec}, kept, late_small, small_out, widths[2], small_out.shape[1]
    )
    partial[...], head_grads, write_grads = backward_part(
        grad_ref[...], total[...], inv[:, 0:1], w_in, w_out, head, same, mask, acts, joined, turn,
        grad_in, grad_out, grad_small, vec_grads, widths, n, grad_in.shape[1]
    )
    write_grads()
    write_heads(head_grads, heads)


def last_step(widths, part_in, other_in, grad, stream, vec, vec_grads, small, result, small_out, kept):
    kept[...] = vec_grads[...]
    result[...] = finish_part(
        part_in[...].astype(F32) + other_in[...].astype(F32), grad[...], stream[...],
        {"vec": vec}, kept, small, small_out, widths[2], small_out.shape[1]
    ).astype(BF16)


def run_blocks(stream_in, cotan_in, segment_ids, live_rows, stacked, head_params):
    same, conv_masks = seq_structure(segment_ids)
    masks = jnp.concatenate(
        [jnp.ones_like(conv_masks[1])] + conv_masks[1:] + [live_rows.astype(F32)], axis=1
    )
    masks = jnp.pad(masks, ((0, 0), (0, SMALL - masks.shape[1])))
    n = lax.axis_size("dp")
    widths = (stacked[0].shape[3], stacked[2].shape[2], stacked[1].shape[2])
    inner_width, state_width, head_count = widths
    rows, model = stream_in.shape
    in_width = 2 * inner_width + state_width
    shard = model // n
    (in_0, out_0), (in_1, out_1) = gather_weights(*pack_weights(stacked), n)
    head_rows = jnp.pad(
        jnp.stack(head_params, axis=1).astype(F32), ((0, 0), (0, 5), (0, SMALL - head_count))
    )
    acts = act_shapes(model, widths)
    wide = shape(rows, model, F32)
    low = shape(rows, model, BF16)
    small = shape(rows, SMALL, F32)
    stream_0, part, square, *acts_0 = call(
        functools.partial(first_forward, widths, n),
        "first_forward",
        (stream_in, in_0, out_0, head_rows[0], same, masks),
        [wide, low, small] + acts,
    )
    stream_1, total_0, inv_0, part_1, square_1, *acts_1 = call(
        functools.partial(next_forward, widths, n),
        "next_forward",
        (stream_0, part, swapped(part, "tensor", 0), square, swapped(square, "tensor", 0), in_1,
         out_1, head_rows[1], same, masks),
        [wide, wide, small, low, small] + acts,
    )
    grads = [
        low,
        jax.ShapeDtypeStruct((n, shard, in_width), BF16),
        jax.ShapeDtypeStruct((n, shard, inner_width), BF16),
        shape(model, SMALL, F32),
        shape(VROWS, model, F32),
        shape(8, SMALL, F32),
    ]
    small_shape = jax.ShapeDtypeStruct((n, shard, SMALL), BF16)
    scratch = [pltpu.VMEM((rows, in_width + SMALL), BF16), pltpu.VMEM((model, rows), BF16)]
    kept = pltpu.VMEM((VROWS, model), F32)
    result, part, grad_in_1, grad_out_1, gs_1, vec_1, heads_1 = call(
        functools.partial(last_backward, widths, n),
        "last_backward",
        (stream_1, part_1, swapped(part_1, "tensor", 0), square_1, swapped(square_1, "tensor", 0),
         cotan_in, in_1, out_1, head_rows[1], same, masks, *acts_1),
        [low] + grads,
        scratch,
    )
    vec_at = [name for name, _, _ in ACTS].index("vec")
    small_1, grad_1, part, grad_in_0, grad_out_0, gs_0, vec_0, heads_0 = call(
        functools.partial(next_backward, widths, n),
        "next_backward",
        (part, swapped(part, "tensor", 0), cotan_in, stream_1, acts_1[vec_at], vec_1, gs_1, total_0,
         inv_0, in_0, out_0, head_rows[0], same, masks, *acts_0),
        [small_shape, wide] + grads,
        scratch + [kept],
    )
    gradient, small_0 = call(
        functools.partial(last_step, widths),
        "last_step",
        (part, swapped(part, "tensor", 0), grad_1, stream_0, acts_0[vec_at], vec_0, gs_0),
        [low, small_shape],
        [kept],
    )
    head_block = jnp.concatenate([heads_0[:3], heads_1[:3], jnp.zeros((2, SMALL), F32)])
    total, head_parts = scatter_grads(
        (grad_in_0, grad_out_0, small_0), (grad_in_1, grad_out_1, small_1), head_block, widths, n
    )
    weight_grads = unpack_grads(total, widths, n)
    head_total = jnp.sum(head_parts, axis=0)[:6, :head_count].reshape(LAYERS, 3, head_count)
    head_grads = tuple(head_total[:, slot_index] for slot_index in range(3))
    return (result, gradient, weight_grads, head_grads)


def body(
    block_input,
    cotangent,
    seq_len,
    norm_gain,
    gate_inner_proj,
    step_proj,
    state_proj,
    conv_inner,
    conv_inner_bias,
    conv_state,
    conv_state_bias,
    step_bias,
    log_rate,
    skip_gain,
    gate_gain,
    out_proj,
):
    home_count = block_input.shape[0]
    own_total = jnp.sum(seq_len)
    live_home = (jnp.arange(home_count, dtype=jnp.int32) < own_total)[:, None]
    stacked = (
        gate_inner_proj,
        step_proj,
        state_proj,
        conv_inner,
        conv_inner_bias,
        conv_state,
        conv_state_bias,
        norm_gain,
        gate_gain,
        out_proj,
    )
    head_params = (step_bias, log_rate, skip_gain)
    partner_bit = lax.axis_size("dp").bit_length() - 2
    partner_len = swapped(seq_len, "dp", partner_bit)
    segment_ids, live_rows, kept_rows = balanced_layout(seq_len, partner_len)
    arrived = swapped(
        (take_rows(block_input, kept_rows, LMAX), take_rows(cotangent, kept_rows, LMAX)),
        "dp",
        partner_bit,
    )
    stream_in = place_rows(block_input, arrived[0], kept_rows, BAL)
    cotan_in = place_rows(cotangent, arrived[1], kept_rows, BAL)
    result, gradient, weight_grads, head_grads = run_blocks(
        stream_in, cotan_in, segment_ids, live_rows, stacked, head_params
    )
    out_rows, grad_rows = result, gradient
    returned = swapped(
        (take_rows(out_rows, kept_rows, LMAX), take_rows(grad_rows, kept_rows, LMAX)),
        "dp",
        partner_bit,
    )
    out_rows = place_rows(out_rows, returned[0], kept_rows, home_count)
    grad_rows = place_rows(grad_rows, returned[1], kept_rows, home_count)
    zero_rows = jnp.zeros_like(out_rows)
    out_rows = jnp.where(live_home, out_rows, zero_rows)
    grad_rows = jnp.where(live_home, grad_rows, zero_rows)
    return (
        out_rows,
        grad_rows,
        weight_grads[7],
        weight_grads[0],
        weight_grads[1],
        weight_grads[2],
        weight_grads[3],
        weight_grads[4],
        weight_grads[5],
        weight_grads[6],
        head_grads[0],
        head_grads[1],
        head_grads[2],
        weight_grads[8],
        weight_grads[9],
    )


def solution(mesh):
    return jax.shard_map(
        body,
        mesh=mesh,
        in_specs=(
            P("dp", None),
            P("dp", None),
            P("dp"),
            P(None, "dp"),
            P(None, "dp", None, "tensor"),
            P(None, "dp", "tensor"),
            P(None, "dp", None),
            P(None, None, ("tensor", "dp")),
            P(None, ("tensor", "dp")),
            P(None, None, "dp"),
            P(None, "dp"),
            P(None, "tensor"),
            P(None, "tensor"),
            P(None, "tensor"),
            P(None, ("tensor", "dp")),
            P(None, "tensor", "dp"),
        ),
        out_specs=(
            P("dp", None),
            P("dp", None),
            P(None, "dp"),
            P(None, "dp", None, "tensor"),
            P(None, "dp", "tensor"),
            P(None, "dp", None),
            P(None, None, ("tensor", "dp")),
            P(None, ("tensor", "dp")),
            P(None, None, "dp"),
            P(None, "dp"),
            P(None, "tensor"),
            P(None, "tensor"),
            P(None, "tensor"),
            P(None, ("tensor", "dp")),
            P(None, "tensor", "dp"),
        ),
        check_vma=False,
    )
```

```python
import functools

import jax
import jax.numpy as jnp
from jax import lax
from jax.experimental import pallas as pl
from jax.experimental.pallas import tpu as pltpu
from jax.sharding import PartitionSpec as P

E = 2048
KERNEL = 4
LAYERS = 2
LMAX = 64
BAL = 128
SMALL = 128


EPSILON = 1e-05
HIGHEST = lax.Precision.HIGHEST


def swapped(array, axis, stride):
    return lax.ppermute(array, axis, [(i, i ^ 1 << stride) for i in range(lax.axis_size(axis))])


MESH = pl.DeviceIdType.MESH


def ring_chip(position, chips):
    half = chips // 2
    position = lax.rem(position + 2 * chips, chips)
    column = position // half
    level = position * (1 - column) + (chips - 1 - position) * column
    return level * 2 + column


def ring_place(chips):
    me = lax.axis_index("dp")
    core = lax.rem(me, 2)
    chip = me // 2
    column = lax.rem(chip, 2)
    level = chip // 2
    position = level * (1 - column) + (chips - 1 - level) * column
    return me, core, position


def remote(src, dst, send_sem, recv_sem, target, axis="dp"):
    return pltpu.make_async_remote_copy(
        src_ref=src,
        dst_ref=dst,
        send_sem=send_sem,
        recv_sem=recv_sem,
        device_id={axis: target},
        device_id_type=MESH,
    )


GROUPS = ((0, 1), (2, 3))


class Gather:
    def __init__(self, n, shards, wholes, ring_send, ring_recv, core_send, core_recv):
        self.n = n
        self.chips = n // 2
        self.reach = self.chips // 2
        self.me, self.core, self.position = ring_place(self.chips)
        self.partner = self.me + 1 - 2 * self.core
        self.sides = (self.device_at(1), self.device_at(-1))
        self.shards, self.wholes = shards, wholes
        self.sems = ring_send, ring_recv, core_send, core_recv
        self.sends = []
        self.steps = []
        self.taken = 0
        self.ends = []
        self.ends = [0] * len(shards)
        ready = [functools.partial(self.begin, phase) for phase in GROUPS[0]]
        self.steps.extend(ready)
        for index, group in enumerate(GROUPS):
            for step in range(1, self.reach + 1):
                if step == self.reach and index + 1 < len(GROUPS):
                    self.steps.extend(
                        functools.partial(self.begin, phase) for phase in GROUPS[index + 1]
                    )
                for phase in group:
                    for half in range(2):
                        for flow in range(2):
                            if half in self.halves(step, flow):
                                self.steps.append(
                                    functools.partial(self.arrive, phase, step, half, flow)
                                )
                    self.ends[phase] = len(self.steps)

    def device_at(self, offset, core=None):
        core = self.core if core is None else core
        return ring_chip(self.position + offset, self.chips) * 2 + core

    def halves(self, step, flow):
        return (flow,) if step == self.reach else (0, 1)

    def columns(self, phase, half):
        width = self.shards[phase].shape[1]
        cut = (width + SMALL) // (2 * SMALL) * SMALL
        return pl.ds(0, cut) if half == 0 else pl.ds(cut, width - cut)

    def place(self, phase, half, slot):
        rows = self.shards[phase].shape[0]
        return self.wholes[phase].at[
            pl.ds(pl.multiple_of(slot * rows, rows), rows), self.columns(phase, half)
        ]

    def ring_copy(self, source, slot, phase, step, half, flow):
        ring_send, ring_recv, _, _ = self.sems
        piece = 2 * phase + half
        return remote(
            source,
            self.place(phase, half, slot),
            ring_send.at[flow, step - 1, piece],
            ring_recv.at[flow, step - 1, piece],
            self.sides[flow],
        )

    def core_copy(self, source, slot, phase, index, half):
        _, _, core_send, core_recv = self.sems
        piece = 2 * phase + half
        return remote(
            source,
            self.place(phase, half, slot),
            core_send.at[index, piece],
            core_recv.at[index, piece],
            self.partner,
        )

    def send(self, copy):
        copy.start()
        self.sends.append(copy)

    def begin(self, phase):
        for half in range(2):
            source = self.shards[phase].at[:, self.columns(phase, half)]
            for flow in range(2):
                if half in self.halves(1, flow):
                    self.send(self.ring_copy(source, self.me, phase, 1, half, flow))
            self.send(self.core_copy(source, self.me, phase, 0, half))
            self.place(phase, half, self.me)[...] = source[...]

    def arrive(self, phase, step, half, flow):
        slot = self.device_at((2 * flow - 1) * step)
        arrived = self.place(phase, half, slot)
        self.ring_copy(arrived, slot, phase, step, half, flow).wait_recv()
        if step < self.reach and half in self.halves(step + 1, flow):
            self.send(self.ring_copy(arrived, slot, phase, step + 1, half, flow))
        self.send(self.core_copy(arrived, slot, phase, 1 + flow * self.reach + step - 1, half))

    def tick(self, count=1):
        for _ in range(count):
            if self.taken < len(self.steps):
                self.steps[self.taken]()
                self.taken += 1

    def need(self, phase):
        self.tick(max(0, self.ends[phase] - self.taken))
        for half in range(2):
            slot = self.partner
            self.core_copy(self.place(phase, half, slot), slot, phase, 0, half).wait_recv()
            for step in range(1, self.reach + 1):
                for flow in range(2):
                    if half in self.halves(step, flow):
                        slot = self.device_at((2 * flow - 1) * step, 1 - self.core)
                        self.core_copy(
                            self.place(phase, half, slot),
                            slot,
                            phase,
                            1 + flow * self.reach + step - 1,
                            half,
                        ).wait_recv()

    def finish(self):
        for copy in self.sends:
            copy.wait_send()


CHUNKS = 4


def forward_kernel(widths, n, in_shard, out_shard, rows_in, heads, same, masks, *rest):
    count = len(ACTS)
    wholes_out, rest = rest[:4], rest[4:]
    stream_0, stream_1, total_0, inv_0, part_1, square_1 = rest[:6]
    acts = named(rest[6 : 6 + count]), named(rest[6 + count : 6 + 2 * count])
    (
        *wholes, part_0, other_0, square_0, other_square, ring_send, ring_recv, core_send,
        core_recv, pair_send, pair_recv, out_sem
    ) = rest[6 + 2 * count :]
    shards = (in_shard.at[0], out_shard.at[0], in_shard.at[1], out_shard.at[1])
    gather = Gather(n, shards, wholes, ring_send, ring_recv, core_send, core_recv)
    across = 1 - lax.axis_index("tensor")
    barrier = pltpu.get_barrier_semaphore()
    for target in (*gather.sides, gather.partner):
        pl.semaphore_signal(barrier, inc=1, device_id={"dp": target}, device_id_type=MESH)
    pl.semaphore_signal(barrier, inc=1, device_id={"tensor": across}, device_id_type=MESH)
    pl.semaphore_wait(barrier, 4)
    gather.tick(len(GROUPS[0]))
    stream_0[...] = live_of(rows_in, masks)
    outs = []

    def need(phase):
        gather.need(phase)
        outs.append(
            pltpu.make_async_copy(wholes[phase], wholes_out[phase], out_sem.at[phase])
        )
        outs[-1].start()

    copies = []

    def send_square(square):
        square_0[...] = square
        copies.append(
            remote(
                square_0, other_square, pair_send.at[CHUNKS], pair_recv.at[CHUNKS], across, "tensor"
            )
        )
        copies[-1].start()

    def send_part(chunk, columns, values):
        part_0[:, columns] = values
        copies.append(
            remote(
                part_0.at[:, columns],
                other_0.at[:, columns],
                pair_send.at[chunk],
                pair_recv.at[chunk],
                across,
                "tensor",
            )
        )
        copies[-1].start()

    need(0)
    forward_part(
        stream_0[...], wholes[0], wholes[1], heads.at[0], same, masks, acts[0], widths, n,
        gather.tick, functools.partial(need, 1), send_square, send_part
    )
    gather.tick(2)
    for copy in copies:
        copy.wait()
    total_0[...], scale = mixed_of(part_0[...], other_0[...], square_0[...], other_square[...])
    inv_0[...] = jnp.broadcast_to(scale, inv_0.shape)
    stream_1[...] = stream_0[...] + total_0[...] * scale
    need(2)

    def keep_square(square):
        square_1[...] = square

    def keep_part(chunk, columns, values):
        part_1[:, columns] = values

    forward_part(
        stream_1[...], wholes[2], wholes[3], heads.at[1], same, masks, acts[1], widths, n,
        gather.tick, functools.partial(need, 3), keep_square, keep_part
    )
    gather.finish()
    for copy in outs:
        copy.wait()


def gather_forward(in_shard, out_shard, rows_in, heads, same, masks, widths, n):
    shard = in_shard.shape[1]
    reach = n // 4
    rows, model = rows_in.shape
    wholes = [
        shape(n * shard, array.shape[2], BF16)
        for array in (in_shard, out_shard, in_shard, out_shard)
    ]
    acts = act_shapes(model, widths)
    outs = [
        shape(rows, model, F32),
        shape(rows, model, F32),
        shape(rows, model, F32),
        shape(rows, SMALL, F32),
        shape(rows, model, BF16),
        shape(rows, SMALL, F32),
    ]
    vmem = pl.BlockSpec(memory_space=pltpu.VMEM)
    results = pl.pallas_call(
        functools.partial(forward_kernel, widths, n),
        out_shape=(*wholes, *outs, *acts, *acts),
        in_specs=[vmem] * 6,
        out_specs=(pl.BlockSpec(memory_space=pl.ANY),) * 4 + (vmem,) * (6 + 2 * len(acts)),
        scratch_shapes=[pltpu.VMEM(whole.shape, BF16) for whole in wholes]
        + [
            pltpu.VMEM((rows, model), BF16),
            pltpu.VMEM((rows, model), BF16),
            pltpu.VMEM((rows, SMALL), F32),
            pltpu.VMEM((rows, SMALL), F32),
            pltpu.SemaphoreType.DMA((2, reach, 8)),
            pltpu.SemaphoreType.DMA((2, reach, 8)),
            pltpu.SemaphoreType.DMA((2 * reach + 1, 8)),
            pltpu.SemaphoreType.DMA((2 * reach + 1, 8)),
            pltpu.SemaphoreType.DMA((CHUNKS + 1,)),
            pltpu.SemaphoreType.DMA((CHUNKS + 1,)),
            pltpu.SemaphoreType.DMA((4,)),
        ],
        compiler_params=pltpu.CompilerParams(
            collective_id=0, has_side_effects=True, vmem_limit_bytes=60 * 1024 * 1024
        ),
        name="gather_forward",
    )(in_shard, out_shard, rows_in, heads, same, masks)
    count = len(acts)
    return results[:4], results[4:10], results[10 : 10 + count], results[10 + count :]


def scatter_kernel(
    n,
    parts,
    up_in,
    up_out,
    up_small,
    down_in,
    down_out,
    down_small,
    head_ref,
    out_ref,
    heads_ref,
    core_up,
    core_down,
    send_buf,
    recv_buf,
    core_send,
    core_recv,
    ring_send,
    ring_recv,
    head_send,
    head_recv,
):
    chips = n // 2
    me, core, position = ring_place(chips)
    partner = me + 1 - 2 * core
    grads = ((up_in, up_out, up_small), (down_in, down_out, down_small))
    cores = (core_up, core_down)

    def device_at(place):
        return ring_chip(place, chips) * 2 + core

    sides = (device_at(position + 1), device_at(position - 1))
    barrier = pltpu.get_barrier_semaphore()

    @pl.loop(1, n)
    def _(k):
        pl.semaphore_signal(
            barrier, inc=1, device_id={"dp": lax.rem(me + k, n)}, device_id_type=MESH
        )

    pl.semaphore_wait(barrier, n - 1)

    def shard_at(flow, step):
        return ring_chip(position + (2 * flow - 1) * step, chips)

    core_copies = {}
    for step in range(1, chips + 1):
        for flow in range(2):
            chip = shard_at(flow, step)
            for part, (array, start, place, size) in enumerate(parts):
                copy = remote(
                    grads[flow][array].at[2 * chip + 1 - core, :, pl.ds(start, size)],
                    cores[flow].at[step - 1, :, pl.ds(place, size)],
                    core_send.at[flow, step - 1, part],
                    core_recv.at[flow, step - 1, part],
                    partner,
                )
                copy.start()
                core_copies[flow, step, part] = copy

    @pl.loop(1, n)
    def _(k):
        remote(
            head_ref,
            heads_ref.at[me],
            head_send.at[k],
            head_recv.at[k],
            lax.rem(me + k, n),
        ).start()

    heads_ref[pl.ds(me, 1)] = head_ref[...][None]

    ring_copies = {}
    for step in range(1, chips + 1):
        for part, (array, start, place, size) in enumerate(parts):
            columns = pl.ds(place, size)
            for flow in range(2):
                own = 2 * shard_at(flow, step) + core
                core_copies[flow, step, part].wait_recv()
                total = grads[flow][array][own, :, pl.ds(start, size)].astype(
                    jnp.float32
                ) + cores[flow][step - 1, :, columns].astype(jnp.float32)
                if step > 1:
                    ring_copies[flow, step - 1, part].wait_recv()
                    total = total + recv_buf[flow, step - 2, :, columns].astype(jnp.float32)
                if step == chips:
                    out_ref[flow, :, columns] = total
                else:
                    send_buf[flow, step - 1, :, columns] = total.astype(jnp.bfloat16)
                    copy = remote(
                        send_buf.at[flow, step - 1, :, columns],
                        recv_buf.at[flow, step - 1, :, columns],
                        ring_send.at[flow, step - 1, part],
                        ring_recv.at[flow, step - 1, part],
                        sides[flow],
                    )
                    copy.start()
                    ring_copies[flow, step, part] = copy
    for copy in core_copies.values():
        copy.wait_send()
    for copy in ring_copies.values():
        copy.wait_send()

    @pl.loop(1, n)
    def _(k):
        sender = lax.rem(me - k + n, n)
        copy = remote(
            head_ref,
            heads_ref.at[sender],
            head_send.at[k],
            head_recv.at[k],
            lax.rem(me + k, n),
        )
        copy.wait_send()
        copy.wait_recv()


def scatter_grads(up, down, heads, widths, n):
    rows = up[0].shape[1]
    in_width = 2 * widths[0] + widths[1]
    out_width = up[1].shape[2]
    chips = n // 2
    cut = in_width // 256 * 128
    parts = (
        (0, 0, 0, cut),
        (0, cut, cut, in_width - cut),
        (1, 0, in_width, out_width),
        (2, 0, in_width + out_width, SMALL),
    )
    width = in_width + out_width + SMALL
    vmem = pl.BlockSpec(memory_space=pltpu.VMEM)
    return pl.pallas_call(
        functools.partial(scatter_kernel, n, parts),
        out_shape=(
            jax.ShapeDtypeStruct((2, rows, width), jnp.float32),
            jax.ShapeDtypeStruct((n,) + heads.shape, jnp.float32),
        ),
        in_specs=[vmem] * 7,
        out_specs=(vmem, vmem),
        scratch_shapes=[
            pltpu.VMEM((chips, rows, width), jnp.bfloat16),
            pltpu.VMEM((chips, rows, width), jnp.bfloat16),
            pltpu.VMEM((2, chips - 1, rows, width), jnp.bfloat16),
            pltpu.VMEM((2, chips - 1, rows, width), jnp.bfloat16),
            pltpu.SemaphoreType.DMA((2, chips, 4)),
            pltpu.SemaphoreType.DMA((2, chips, 4)),
            pltpu.SemaphoreType.DMA((2, chips - 1, 4)),
            pltpu.SemaphoreType.DMA((2, chips - 1, 4)),
            pltpu.SemaphoreType.DMA((n,)),
            pltpu.SemaphoreType.DMA((n,)),
        ],
        compiler_params=pltpu.CompilerParams(
            collective_id=1, has_side_effects=True, vmem_limit_bytes=60 * 1024 * 1024
        ),
        name="scatter_grads",
    )(*up, *down, heads)


F32 = jnp.float32
BF16 = jnp.bfloat16
VROWS = 16
NN = (((1,), (0,)), ((), ()))
NT = (((1,), (1,)), ((), ()))
TN = (((0,), (0,)), ((), ()))


def mul(a, b, dims=NN):
    return lax.dot_general(
        a.astype(BF16), b.astype(BF16), dims, preferred_element_type=F32
    )


def mul_wide(a, b, dims=NN):
    return lax.dot_general(a, b, dims, precision=HIGHEST, preferred_element_type=F32)


def mul_split(a, b, dims=NN):
    high = a.astype(BF16)
    low = (a - high.astype(F32)).astype(BF16)
    return mul(high, b, dims) + mul(low, b, dims)


def iota(shape, axis):
    return lax.broadcasted_iota(jnp.int32, shape, axis)


def one_hot(mask):
    return jnp.where(mask, 1.0, 0.0).astype(BF16)


def row_picker(head_count):
    shape = (VROWS, SMALL)
    return one_hot(iota(shape, 0) + head_count == iota(shape, 1))


def state_picker(model, state_width, n):
    per_device = state_width // n
    shape = (model, state_width)
    column = iota(shape, 1)
    owner = lax.shift_right_logical(column, per_device.bit_length() - 1)
    return one_hot(
        iota(shape, 0) == owner * (model // n) + jnp.bitwise_and(column, per_device - 1)
    )


def head_picker(inner_width, head_count):
    head_size = inner_width // head_count
    shape = (inner_width, SMALL)
    return one_hot(
        lax.shift_right_logical(iota(shape, 0), head_size.bit_length() - 1) == iota(shape, 1)
    )


def slope_of(values):
    sigmoid_val = jax.nn.sigmoid(values)
    return sigmoid_val * (1.0 + values * (1.0 - sigmoid_val))


def softplus(values):
    return jnp.maximum(values, 0.0) + jnp.log1p(jnp.exp(-jnp.abs(values)))


def causal_conv(raw, taps, bias, masks):
    total = bias + taps[KERNEL - 1 : KERNEL] * raw
    for lag in range(1, KERNEL):
        tap = KERNEL - 1 - lag
        total = total + taps[tap : tap + 1] * (pltpu.roll(raw, lag, 0) * masks[:, lag : lag + 1])
    return total


def causal_conv_back(grad, raw, taps, masks):
    rows = grad.shape[0]
    tap_grads = [None] * KERNEL
    tap_grads[KERNEL - 1] = jnp.sum(grad * raw, axis=0, keepdims=True)
    source = taps[KERNEL - 1 : KERNEL] * grad
    for lag in range(1, KERNEL):
        tap = KERNEL - 1 - lag
        masked = grad * masks[:, lag : lag + 1]
        tap_grads[tap] = jnp.sum(masked * pltpu.roll(raw, lag, 0), axis=0, keepdims=True)
        source = source + taps[tap : tap + 1] * pltpu.roll(masked, rows - lag, 0)
    return tap_grads + [jnp.sum(grad, axis=0, keepdims=True)], source


def row_scale(stream):
    return lax.rsqrt(jnp.mean(stream * stream, axis=1, keepdims=True) + EPSILON)


def pair_blocks(head_count, inner_width):
    head_size = inner_width // head_count
    per_block = SMALL // head_size
    return [
        (slice(block * SMALL, (block + 1) * SMALL), range(block * per_block, (block + 1) * per_block))
        for block in range(inner_width // SMALL)
    ]


def spread(columns, heads, head_size):
    rows = columns.shape[0]
    lane_head = lax.shift_right_logical(iota((rows, SMALL), 1), head_size.bit_length() - 1)
    total = columns[:, heads[0] : heads[0] + 1]
    for place in range(1, len(heads)):
        total = jnp.where(lane_head >= place, columns[:, heads[place] : heads[place] + 1], total)
    return jnp.broadcast_to(total, (rows, SMALL))


def head_lanes(rows, head_size, place):
    lane_head = lax.shift_right_logical(iota((rows, SMALL), 1), head_size.bit_length() - 1)
    return lane_head == place


def decay_of(cum, cum_t, head, inside):
    diff = cum[:, head : head + 1] - cum_t[head : head + 1, :]
    return jnp.exp(jnp.where(inside, diff, -1e30))


ACTS = (
    ("normed", BF16, "model"),
    ("gate_pre", F32, "inner"),
    ("inner_raw", F32, "inner"),
    ("inner_pre", F32, "inner"),
    ("ssm", F32, "inner"),
    ("state_raw", F32, "state"),
    ("state_pre", F32, "state"),
    ("step_raw", F32, "small"),
    ("cum", F32, "small"),
    ("vec", F32, "model"),
    ("vec_state", F32, "state"),
)


def act_shapes(model, widths):
    inner_width, state_width, _ = widths
    width_of = {"model": model, "inner": inner_width, "state": state_width, "small": SMALL}
    return [
        jax.ShapeDtypeStruct(
            (VROWS if name.startswith("vec") else BAL, width_of[kind]), dtype
        )
        for name, dtype, kind in ACTS
    ]


def named(refs):
    return dict(zip([name for name, _, _ in ACTS], refs))


def forward_part(
    stream, w_in, w_out, head_ref, same_ref, mask_ref, acts, widths, n, tick, need_out, on_square,
    on_part
):
    inner_width, state_width, head_count = widths
    model = stream.shape[1]
    rows = stream.shape[0]
    head_size = inner_width // head_count
    half = state_width // 2
    at_state = 2 * inner_width
    at_small = at_state + state_width
    masks = mask_ref[...]
    inside = same_ref[...] > 0.5
    vec = mul(row_picker(head_count), w_in[:, at_small : at_small + SMALL], NT)
    vec_state = mul(vec, state_picker(model, state_width, n))
    acts["vec"][...] = vec
    acts["vec_state"][...] = vec_state
    normed = (stream * row_scale(stream) * vec[0:1]).astype(BF16)
    acts["normed"][...] = normed
    state_step = mul(normed, w_in[:, at_state : at_small + SMALL])
    state_raw = state_step[:, :state_width]
    step_raw = state_step[:, state_width:] + head_ref[0:1]
    acts["state_raw"][...] = state_raw
    acts["step_raw"][...] = step_raw
    tick()
    state_pre = causal_conv(state_raw, vec_state[7:11], vec_state[11:12], masks)
    acts["state_pre"][...] = state_pre
    state = state_pre * jax.nn.sigmoid(state_pre)
    step = softplus(step_raw)
    rate = -jnp.exp(head_ref[1:2])
    cum = mul_wide(same_ref[...], step * rate)
    acts["cum"][...] = cum
    cum_t = cum.T
    intersection = mul(state[:, half:], state[:, :half], NT)
    tick()
    inner_raw = mul(normed, w_in[:, inner_width:at_state])
    acts["inner_raw"][...] = inner_raw
    inner_pre = causal_conv(inner_raw, vec[1:5], vec[5:6], masks)
    acts["inner_pre"][...] = inner_pre
    tick()
    gate_pre = mul(normed, w_in[:, :inner_width])
    acts["gate_pre"][...] = gate_pre
    skip = head_ref[2:3]
    pieces = []
    square = jnp.zeros((rows, 1), F32)
    for block, (lanes, heads) in enumerate(pair_blocks(head_count, inner_width)):
        if block % 2 == 0:
            tick()
        pre = inner_pre[:, lanes]
        inner = pre * jax.nn.sigmoid(pre)
        scaled = (inner * spread(step, heads, head_size)).astype(BF16)
        out = spread(skip, heads, head_size) * inner
        for place, head in enumerate(heads):
            mixer = decay_of(cum, cum_t, head, inside) * intersection
            out = out + jnp.where(head_lanes(rows, head_size, place), mul(mixer, scaled), 0.0)
        acts["ssm"][:, lanes] = out
        gate = gate_pre[:, lanes]
        gated = out * gate * jax.nn.sigmoid(gate)
        square = square + jnp.sum(gated * gated, axis=1, keepdims=True)
        pieces.append((gated * vec[6:7, lanes]).astype(BF16))
    on_square(jnp.broadcast_to(square, (rows, SMALL)))
    need_out()
    gated_low = jnp.concatenate(pieces, axis=1)
    for chunk in range(CHUNKS):
        columns = slice(chunk * model // CHUNKS, (chunk + 1) * model // CHUNKS)
        on_part(chunk, columns, mul(gated_low, w_out[columns], NT).astype(BF16))


def mixed_of(part, other, square, other_square):
    total = part.astype(F32) + other.astype(F32)
    return total, lax.rsqrt((square + other_square)[:, 0:1] / E + EPSILON)


def backward_part(
    grad, total, inv_gate, w_in, w_out, head_ref, same_ref, mask_ref, acts, joined_ref, turn_ref,
    grad_in, grad_out, grad_small, vec_grads, widths, n, shard
):
    inner_width, state_width, head_count = widths
    rows, model = grad.shape
    head_size = inner_width // head_count
    half = state_width // 2
    at_state = 2 * inner_width
    at_small = at_state + state_width
    masks = mask_ref[...]
    inside = same_ref[...] > 0.5
    vec = acts["vec"][...]
    vec_state = acts["vec_state"][...]
    grad_low = grad.astype(BF16)
    inner_sum = jnp.sum(grad_low.astype(F32) * total, axis=1, keepdims=True)
    pull = inv_gate * inv_gate * inv_gate * inner_sum / E
    step_raw = acts["step_raw"][...]
    step = softplus(step_raw)
    rate = -jnp.exp(head_ref[1:2])
    skip = head_ref[2:3]
    cum = acts["cum"][...]
    cum_t = cum.T
    state_pre = acts["state_pre"][...]
    state = state_pre * jax.nn.sigmoid(state_pre)
    intersection = mul(state[:, half:], state[:, :half], NT)
    d_gate_normed = mul(grad_low, w_out[...])
    d_intersection = jnp.zeros((rows, rows), F32)
    row_part = jnp.zeros((rows, SMALL), F32)
    column_part = jnp.zeros((SMALL, rows), F32)
    head_lane = iota((rows, SMALL), 1)
    head_row = iota((SMALL, rows), 0)
    gain_grads = []
    skip_parts = []
    step_parts = []
    inner_taps = []
    gate_pieces = []
    for lanes, heads in pair_blocks(head_count, inner_width):
        pre = acts["inner_pre"][:, lanes]
        sigmoid_inner = jax.nn.sigmoid(pre)
        inner = pre * sigmoid_inner
        gate = acts["gate_pre"][:, lanes]
        gate_sig = jax.nn.sigmoid(gate)
        ssm = acts["ssm"][:, lanes]
        act = gate * gate_sig
        gated = ssm * act
        gain = vec[6:7, lanes]
        d_normed = d_gate_normed[:, lanes]
        gain_grads.append(jnp.sum(d_normed * gated * inv_gate, axis=0, keepdims=True))
        gate_pieces.append((gated * inv_gate * gain).astype(BF16))
        d_gated = inv_gate * gain * d_normed - gated * pull
        d_ssm = d_gated * act
        joined_ref[:, lanes] = (
            d_gated * ssm * gate_sig * (1.0 + gate * (1.0 - gate_sig))
        ).astype(BF16)
        skip_parts.append(jnp.sum(d_ssm * inner, axis=0, keepdims=True))
        step_wide = spread(step, heads, head_size)
        scaled = (inner * step_wide).astype(BF16)
        d_low = d_ssm.astype(BF16)
        d_scaled = jnp.zeros((rows, SMALL), F32)
        for place, head in enumerate(heads):
            mine = head_lanes(rows, head_size, place)
            decay = decay_of(cum, cum_t, head, inside)
            mixer = decay * intersection
            d_scaled = d_scaled + jnp.where(mine, mul(mixer, d_low, TN), 0.0)
            d_mixer = mul(jnp.where(mine, d_ssm, 0.0), scaled, NT)
            d_decayed = d_mixer * decay
            d_intersection = d_intersection + d_decayed
            flow = d_decayed * intersection
            row_part = jnp.where(
                head_lane == head, jnp.sum(flow, axis=1, keepdims=True), row_part
            )
            column_part = jnp.where(
                head_row == head, jnp.sum(flow, axis=0, keepdims=True), column_part
            )
        step_parts.append(d_scaled * inner)
        d_inner = spread(skip, heads, head_size) * d_ssm + d_scaled * step_wide
        d_pre = d_inner * (sigmoid_inner * (1.0 + pre * (1.0 - sigmoid_inner)))
        taps, d_raw = causal_conv_back(
            d_pre, acts["inner_raw"][:, lanes], vec[1:5, lanes], masks
        )
        inner_taps.append(taps)
        joined_ref[:, slice(inner_width + lanes.start, inner_width + lanes.stop)] = d_raw.astype(
            BF16
        )
    gate_normed = jnp.concatenate(gate_pieces, axis=1)
    d_log = mul_wide(same_ref[...], row_part - column_part.T, TN)
    picker = head_picker(inner_width, head_count)
    d_step = mul_split(jnp.concatenate(step_parts, axis=1), picker) + d_log * rate
    d_step_raw = jnp.where(head_lane < head_count, d_step * jax.nn.sigmoid(step_raw), 0.0)
    skip_row = jnp.broadcast_to(jnp.concatenate(skip_parts, axis=1), (8, inner_width))
    head_grads = (
        jnp.sum(d_step_raw, axis=0, keepdims=True),
        jnp.sum(d_log * step, axis=0, keepdims=True) * rate,
        mul_split(skip_row, picker)[0:1],
    )
    d_state = jnp.concatenate(
        [mul(d_intersection, state[:, half:], TN), mul(d_intersection, state[:, :half])], axis=1
    )
    state_taps, d_state_raw = causal_conv_back(
        d_state * slope_of(state_pre), acts["state_raw"][...], vec_state[7:11], masks
    )
    joined_ref[:, at_state:at_small] = d_state_raw.astype(BF16)
    joined_ref[:, at_small : at_small + SMALL] = d_step_raw.astype(BF16)
    partial = mul(joined_ref[...], w_in[...], NT).astype(BF16)
    state_rows = jnp.concatenate(
        [jnp.zeros((7, state_width), F32)]
        + state_taps
        + [jnp.zeros((VROWS - 12, state_width), F32)]
    )
    vec_grads[...] = mul(state_rows, state_picker(model, state_width, n), NT)
    vec_grads[1:7] = jnp.concatenate(
        [
            jnp.concatenate([taps[row] for taps in inner_taps], axis=1)
            for row in range(KERNEL + 1)
        ]
        + [jnp.concatenate(gain_grads, axis=1)]
    )

    def write_grads():
        turn_ref[...] = acts["normed"][...].astype(F32).T.astype(BF16)
        per = SMALL // shard
        for block in range(model // SMALL):
            mine = slice(block * SMALL, (block + 1) * SMALL)
            product = mul(turn_ref[mine], joined_ref[...])
            grad_in[block * per : (block + 1) * per] = product[:, :at_small].reshape(
                per, shard, at_small
            ).astype(BF16)
            grad_small[mine] = product[:, at_small:]
        turn_ref[...] = grad.T.astype(BF16)
        for block in range(model // SMALL):
            mine = slice(block * SMALL, (block + 1) * SMALL)
            grad_out[block * per : (block + 1) * per] = (
                mul(turn_ref[mine], gate_normed).reshape(per, shard, inner_width).astype(BF16)
            )

    return partial, head_grads, write_grads


def finish_part(d_normed, grad, stream, acts, vec_grads, grad_small, small_out, head_count, shard):
    model = stream.shape[1]
    inv_rms = row_scale(stream)
    vec_grads[0:1] = jnp.sum(d_normed * stream * inv_rms, axis=0, keepdims=True)
    small = grad_small[...] + mul(vec_grads[...], row_picker(head_count), TN)
    small_out[...] = small.reshape(model // shard, shard, SMALL).astype(BF16)
    scaled = d_normed * acts["vec"][0:1]
    return (
        grad
        + inv_rms * scaled
        - stream
        * (inv_rms * inv_rms * inv_rms)
        * jnp.sum(scaled * stream, axis=1, keepdims=True)
        / model
    )


def running_sum(lengths):
    index = jnp.arange(lengths.shape[0], dtype=jnp.int32)
    return jnp.sum(jnp.where(index[:, None] >= index[None, :], lengths[None, :], 0), axis=1)


def segments_of(lengths, row_total):
    ends = running_sum(lengths)
    position = jnp.arange(row_total, dtype=jnp.int32)
    return jnp.sum((position[:, None] >= ends[None, :]).astype(jnp.int32), axis=1)


def seq_structure(segment_ids):
    row_total = segment_ids.shape[0]
    position = jnp.arange(row_total, dtype=jnp.int32)
    same_seq = (
        (segment_ids[:, None] == segment_ids[None, :]) & (position[:, None] >= position[None, :])
    ).astype(jnp.float32)
    conv_masks = [None]
    for lag_rows in range(1, KERNEL):
        earlier = jnp.concatenate([jnp.full((lag_rows,), -1, jnp.int32), segment_ids[:-lag_rows]])
        conv_masks.append((segment_ids == earlier).astype(jnp.float32)[:, None])
    return (same_seq, conv_masks)


def take_rows(buffer, start_row, row_count):
    padding = jnp.zeros((row_count, buffer.shape[1]), buffer.dtype)
    return lax.dynamic_slice_in_dim(
        jnp.concatenate([buffer, padding], axis=0), start_row, row_count, 0
    )


def place_rows(own_rows, arrived, kept_rows, rows_out):
    row_width = own_rows.shape[1]
    if own_rows.shape[0] >= rows_out:
        base_rows = own_rows[:rows_out]
    else:
        base_rows = jnp.concatenate(
            [own_rows, jnp.zeros((rows_out - own_rows.shape[0], row_width), own_rows.dtype)], axis=0
        )
    extended = jnp.concatenate(
        [
            jnp.zeros((rows_out, row_width), own_rows.dtype),
            arrived,
            jnp.zeros((rows_out - arrived.shape[0], row_width), own_rows.dtype),
        ],
        axis=0,
    )
    moved_rows = lax.dynamic_slice_in_dim(extended, rows_out - kept_rows, rows_out, 0)
    position = jnp.arange(rows_out, dtype=jnp.int32)
    return jnp.where((position < kept_rows)[:, None], base_rows, moved_rows)


def balanced_layout(own_len, partner_len):
    own_end = running_sum(own_len)
    keep_flag = (own_end <= BAL).astype(jnp.int32)
    kept_rows = jnp.sum(own_len * keep_flag)
    partner_end = running_sum(partner_len)
    incoming = partner_len * (partner_end > BAL).astype(jnp.int32)
    segment_ids = segments_of(jnp.concatenate([own_len * keep_flag, incoming]), BAL)
    live_rows = (jnp.arange(BAL, dtype=jnp.int32) < kept_rows + jnp.sum(incoming))[:, None]
    return (segment_ids, live_rows, kept_rows)


def pad_rows(array, rows):
    return jnp.pad(array, ((0, 0), (0, rows - array.shape[1]), (0, 0)))


def pack_weights(stacked):
    (
        gate_inner_proj,
        step_proj,
        state_proj,
        conv_inner,
        conv_inner_bias,
        conv_state,
        conv_state_bias,
        norm_gain,
        gate_gain,
        out_proj,
    ) = stacked
    layers, rows = norm_gain.shape
    columns = [
        step_proj,
        norm_gain[:, :, None],
        jnp.swapaxes(conv_inner, 1, 2),
        conv_inner_bias[:, :, None],
        gate_gain[:, :, None],
        pad_rows(jnp.swapaxes(conv_state, 1, 2), rows),
        pad_rows(conv_state_bias[:, :, None], rows),
    ]
    used = sum(column.shape[2] for column in columns)
    columns.append(jnp.zeros((layers, rows, SMALL - used), norm_gain.dtype))
    in_shard = jnp.concatenate(
        [gate_inner_proj.reshape(layers, rows, -1), state_proj] + columns, axis=2
    )
    return in_shard, jnp.swapaxes(out_proj, 1, 2)


def unpack_grads(total, widths, n):
    inner_width, state_width, head_count = widths
    layers, rows = total.shape[:2]
    in_width = 2 * inner_width + state_width
    per_device = state_width // n
    small = total[:, :, total.shape[2] - SMALL :]
    step = small[:, :, :head_count]
    small = small[:, :, head_count : head_count + 12]
    shared = jnp.concatenate(
        [total[:, :, 2 * inner_width : in_width], jnp.pad(small[:, :, 7:12], ((0, 0), (0, 0), (0, SMALL - 5)))],
        axis=2,
    )
    shared = shared + swapped(shared, "tensor", 0)
    state = shared[:, :per_device, state_width:]
    return (
        total[:, :, : 2 * inner_width].reshape(layers, rows, 2, inner_width),
        step,
        shared[:, :, :state_width],
        jnp.swapaxes(small[:, :, 1:5], 1, 2),
        small[:, :, 5],
        jnp.swapaxes(state[:, :, :KERNEL], 1, 2),
        state[:, :, KERNEL],
        small[:, :, 0],
        small[:, :, 6],
        jnp.swapaxes(total[:, :, in_width : total.shape[2] - SMALL], 1, 2),
    )


def call(body, name, operands, outs, scratch=()):
    vmem = pl.BlockSpec(memory_space=pltpu.VMEM)
    return pl.pallas_call(
        body,
        out_shape=tuple(outs),
        in_specs=[vmem] * len(operands),
        out_specs=(vmem,) * len(outs),
        scratch_shapes=list(scratch),
        compiler_params=pltpu.CompilerParams(vmem_limit_bytes=56 * 1024 * 1024),
        name=name,
    )(*operands)


def shape(rows, columns, dtype):
    return jax.ShapeDtypeStruct((rows, columns), dtype)


def live_of(values, mask_ref):
    return jnp.where(mask_ref[:, KERNEL : KERNEL + 1] > 0.5, values[...].astype(F32), 0.0)


def write_heads(head_grads, heads):
    for row, grads in enumerate(head_grads):
        heads[row : row + 1] = grads
    heads[len(head_grads) :] = jnp.zeros((8 - len(head_grads), SMALL), F32)


def last_backward(
    widths, n, before, part_in, other_in, square_in, other_square, rows_in, w_in, w_out, head, same,
    mask, *rest
):
    acts, rest = named(rest[: len(ACTS)]), rest[len(ACTS) :]
    result, partial, grad_in, grad_out, grad_small, vec_grads, heads, joined, turn = rest
    total, scale = mixed_of(part_in[...], other_in[...], square_in[...], other_square[...])
    result[...] = (before[...] + total * scale).astype(BF16)
    partial[...], head_grads, write_grads = backward_part(
        live_of(rows_in, mask), total, scale, w_in, w_out, head, same, mask, acts, joined, turn,
        grad_in, grad_out, grad_small, vec_grads, widths, n, grad_in.shape[1]
    )
    write_grads()
    write_heads(head_grads, heads)


def next_backward(
    widths, n, part_in, other_in, rows_in, stream, late_vec, late_vec_grads, late_small, total, inv,
    w_in, w_out, head, same, mask, *rest
):
    acts, rest = named(rest[: len(ACTS)]), rest[len(ACTS) :]
    (
        small_out, grad_ref, partial, grad_in, grad_out, grad_small, vec_grads, heads, joined, turn,
        kept
    ) = rest
    kept[...] = late_vec_grads[...]
    grad_ref[...] = finish_part(
        part_in[...].astype(F32) + other_in[...].astype(F32), live_of(rows_in, mask), stream[...],
        {"vec": late_vec}, kept, late_small, small_out, widths[2], small_out.shape[1]
    )
    partial[...], head_grads, write_grads = backward_part(
        grad_ref[...], total[...], inv[:, 0:1], w_in, w_out, head, same, mask, acts, joined, turn,
        grad_in, grad_out, grad_small, vec_grads, widths, n, grad_in.shape[1]
    )
    write_grads()
    write_heads(head_grads, heads)


def last_step(widths, part_in, other_in, grad, stream, vec, vec_grads, small, result, small_out, kept):
    kept[...] = vec_grads[...]
    result[...] = finish_part(
        part_in[...].astype(F32) + other_in[...].astype(F32), grad[...], stream[...],
        {"vec": vec}, kept, small, small_out, widths[2], small_out.shape[1]
    ).astype(BF16)


def run_blocks(stream_in, cotan_in, segment_ids, live_rows, stacked, head_params):
    same, conv_masks = seq_structure(segment_ids)
    masks = jnp.concatenate(
        [jnp.ones_like(conv_masks[1])] + conv_masks[1:] + [live_rows.astype(F32)], axis=1
    )
    masks = jnp.pad(masks, ((0, 0), (0, SMALL - masks.shape[1])))
    n = lax.axis_size("dp")
    widths = (stacked[0].shape[3], stacked[2].shape[2], stacked[1].shape[2])
    inner_width, state_width, head_count = widths
    rows, model = stream_in.shape
    in_width = 2 * inner_width + state_width
    shard = model // n
    head_rows = jnp.pad(
        jnp.stack(head_params, axis=1).astype(F32), ((0, 0), (0, 5), (0, SMALL - head_count))
    )
    wide = shape(rows, model, F32)
    low = shape(rows, model, BF16)
    wholes, kept_rows, acts_0, acts_1 = gather_forward(
        *pack_weights(stacked), stream_in, head_rows, same, masks, widths, n
    )
    in_0, out_0, in_1, out_1 = wholes
    stream_0, stream_1, total_0, inv_0, part_1, square_1 = kept_rows
    grads = [
        low,
        jax.ShapeDtypeStruct((n, shard, in_width), BF16),
        jax.ShapeDtypeStruct((n, shard, inner_width), BF16),
        shape(model, SMALL, F32),
        shape(VROWS, model, F32),
        shape(8, SMALL, F32),
    ]
    small_shape = jax.ShapeDtypeStruct((n, shard, SMALL), BF16)
    scratch = [pltpu.VMEM((rows, in_width + SMALL), BF16), pltpu.VMEM((model, rows), BF16)]
    kept = pltpu.VMEM((VROWS, model), F32)
    result, part, grad_in_1, grad_out_1, gs_1, vec_1, heads_1 = call(
        functools.partial(last_backward, widths, n),
        "last_backward",
        (stream_1, part_1, swapped(part_1, "tensor", 0), square_1, swapped(square_1, "tensor", 0),
         cotan_in, in_1, out_1, head_rows[1], same, masks, *acts_1),
        [low] + grads,
        scratch,
    )
    vec_at = [name for name, _, _ in ACTS].index("vec")
    small_1, grad_1, part, grad_in_0, grad_out_0, gs_0, vec_0, heads_0 = call(
        functools.partial(next_backward, widths, n),
        "next_backward",
        (part, swapped(part, "tensor", 0), cotan_in, stream_1, acts_1[vec_at], vec_1, gs_1, total_0,
         inv_0, in_0, out_0, head_rows[0], same, masks, *acts_0),
        [small_shape, wide] + grads,
        scratch + [kept],
    )
    gradient, small_0 = call(
        functools.partial(last_step, widths),
        "last_step",
        (part, swapped(part, "tensor", 0), grad_1, stream_0, acts_0[vec_at], vec_0, gs_0),
        [low, small_shape],
        [kept],
    )
    head_block = jnp.concatenate([heads_0[:3], heads_1[:3], jnp.zeros((2, SMALL), F32)])
    total, head_parts = scatter_grads(
        (grad_in_0, grad_out_0, small_0), (grad_in_1, grad_out_1, small_1), head_block, widths, n
    )
    weight_grads = unpack_grads(total, widths, n)
    head_total = jnp.sum(head_parts, axis=0)[:6, :head_count].reshape(LAYERS, 3, head_count)
    head_grads = tuple(head_total[:, slot_index] for slot_index in range(3))
    return (result, gradient, weight_grads, head_grads)


def body(
    block_input,
    cotangent,
    seq_len,
    norm_gain,
    gate_inner_proj,
    step_proj,
    state_proj,
    conv_inner,
    conv_inner_bias,
    conv_state,
    conv_state_bias,
    step_bias,
    log_rate,
    skip_gain,
    gate_gain,
    out_proj,
):
    home_count = block_input.shape[0]
    own_total = jnp.sum(seq_len)
    live_home = (jnp.arange(home_count, dtype=jnp.int32) < own_total)[:, None]
    stacked = (
        gate_inner_proj,
        step_proj,
        state_proj,
        conv_inner,
        conv_inner_bias,
        conv_state,
        conv_state_bias,
        norm_gain,
        gate_gain,
        out_proj,
    )
    head_params = (step_bias, log_rate, skip_gain)
    partner_bit = lax.axis_size("dp").bit_length() - 2
    partner_len = swapped(seq_len, "dp", partner_bit)
    segment_ids, live_rows, kept_rows = balanced_layout(seq_len, partner_len)
    arrived = swapped(
        (take_rows(block_input, kept_rows, LMAX), take_rows(cotangent, kept_rows, LMAX)),
        "dp",
        partner_bit,
    )
    stream_in = place_rows(block_input, arrived[0], kept_rows, BAL)
    cotan_in = place_rows(cotangent, arrived[1], kept_rows, BAL)
    result, gradient, weight_grads, head_grads = run_blocks(
        stream_in, cotan_in, segment_ids, live_rows, stacked, head_params
    )
    out_rows, grad_rows = result, gradient
    returned = swapped(
        (take_rows(out_rows, kept_rows, LMAX), take_rows(grad_rows, kept_rows, LMAX)),
        "dp",
        partner_bit,
    )
    out_rows = place_rows(out_rows, returned[0], kept_rows, home_count)
    grad_rows = place_rows(grad_rows, returned[1], kept_rows, home_count)
    zero_rows = jnp.zeros_like(out_rows)
    out_rows = jnp.where(live_home, out_rows, zero_rows)
    grad_rows = jnp.where(live_home, grad_rows, zero_rows)
    return (
        out_rows,
        grad_rows,
        weight_grads[7],
        weight_grads[0],
        weight_grads[1],
        weight_grads[2],
        weight_grads[3],
        weight_grads[4],
        weight_grads[5],
        weight_grads[6],
        head_grads[0],
        head_grads[1],
        head_grads[2],
        weight_grads[8],
        weight_grads[9],
    )


def solution(mesh):
    return jax.shard_map(
        body,
        mesh=mesh,
        in_specs=(
            P("dp", None),
            P("dp", None),
            P("dp"),
            P(None, "dp"),
            P(None, "dp", None, "tensor"),
            P(None, "dp", "tensor"),
            P(None, "dp", None),
            P(None, None, ("tensor", "dp")),
            P(None, ("tensor", "dp")),
            P(None, None, "dp"),
            P(None, "dp"),
            P(None, "tensor"),
            P(None, "tensor"),
            P(None, "tensor"),
            P(None, ("tensor", "dp")),
            P(None, "tensor", "dp"),
        ),
        out_specs=(
            P("dp", None),
            P("dp", None),
            P(None, "dp"),
            P(None, "dp", None, "tensor"),
            P(None, "dp", "tensor"),
            P(None, "dp", None),
            P(None, None, ("tensor", "dp")),
            P(None, ("tensor", "dp")),
            P(None, None, "dp"),
            P(None, "dp"),
            P(None, "tensor"),
            P(None, "tensor"),
            P(None, "tensor"),
            P(None, ("tensor", "dp")),
            P(None, "tensor", "dp"),
        ),
        check_vma=False,
    )
```

```python
import functools

import jax
import jax.numpy as jnp
from jax import lax
from jax.experimental import pallas as pl
from jax.experimental.pallas import tpu as pltpu
from jax.sharding import PartitionSpec as P

E = 2048
KERNEL = 4
LAYERS = 2
LMAX = 64
BAL = 128
SMALL = 128


EPSILON = 1e-05
HIGHEST = lax.Precision.HIGHEST


def swapped(array, axis, stride):
    return lax.ppermute(array, axis, [(i, i ^ 1 << stride) for i in range(lax.axis_size(axis))])


MESH = pl.DeviceIdType.MESH


def ring_chip(position, chips):
    half = chips // 2
    position = lax.rem(position + 2 * chips, chips)
    column = position // half
    level = position * (1 - column) + (chips - 1 - position) * column
    return level * 2 + column


def ring_place(chips):
    me = lax.axis_index("dp")
    core = lax.rem(me, 2)
    chip = me // 2
    column = lax.rem(chip, 2)
    level = chip // 2
    position = level * (1 - column) + (chips - 1 - level) * column
    return me, core, position


def remote(src, dst, send_sem, recv_sem, target, axis="dp"):
    return pltpu.make_async_remote_copy(
        src_ref=src,
        dst_ref=dst,
        send_sem=send_sem,
        recv_sem=recv_sem,
        device_id={axis: target},
        device_id_type=MESH,
    )


GROUPS = ((0, 1), (2, 3))


class Gather:
    def __init__(self, n, shards, wholes, ring_send, ring_recv, core_send, core_recv):
        self.n = n
        self.chips = n // 2
        self.reach = self.chips // 2
        self.me, self.core, self.position = ring_place(self.chips)
        self.partner = self.me + 1 - 2 * self.core
        self.sides = (self.device_at(1), self.device_at(-1))
        self.shards, self.wholes = shards, wholes
        self.sems = ring_send, ring_recv, core_send, core_recv
        self.sends = []
        self.steps = []
        self.taken = 0
        self.ends = []
        self.ends = [0] * len(shards)
        ready = [functools.partial(self.begin, phase) for phase in GROUPS[0]]
        self.steps.extend(ready)
        for index, group in enumerate(GROUPS):
            for step in range(1, self.reach + 1):
                if step == self.reach and index + 1 < len(GROUPS):
                    self.steps.extend(
                        functools.partial(self.begin, phase) for phase in GROUPS[index + 1]
                    )
                for phase in group:
                    for half in range(2):
                        for flow in range(2):
                            if half in self.halves(step, flow):
                                self.steps.append(
                                    functools.partial(self.arrive, phase, step, half, flow)
                                )
                    self.ends[phase] = len(self.steps)

    def device_at(self, offset, core=None):
        core = self.core if core is None else core
        return ring_chip(self.position + offset, self.chips) * 2 + core

    def halves(self, step, flow):
        return (flow,) if step == self.reach else (0, 1)

    def columns(self, phase, half):
        width = self.shards[phase].shape[1]
        cut = (width + SMALL) // (2 * SMALL) * SMALL
        return pl.ds(0, cut) if half == 0 else pl.ds(cut, width - cut)

    def place(self, phase, half, slot):
        rows = self.shards[phase].shape[0]
        return self.wholes[phase].at[
            pl.ds(pl.multiple_of(slot * rows, rows), rows), self.columns(phase, half)
        ]

    def ring_copy(self, source, slot, phase, step, half, flow):
        ring_send, ring_recv, _, _ = self.sems
        piece = 2 * phase + half
        return remote(
            source,
            self.place(phase, half, slot),
            ring_send.at[flow, step - 1, piece],
            ring_recv.at[flow, step - 1, piece],
            self.sides[flow],
        )

    def core_copy(self, source, slot, phase, index, half):
        _, _, core_send, core_recv = self.sems
        piece = 2 * phase + half
        return remote(
            source,
            self.place(phase, half, slot),
            core_send.at[index, piece],
            core_recv.at[index, piece],
            self.partner,
        )

    def send(self, copy):
        copy.start()
        self.sends.append(copy)

    def begin(self, phase):
        for half in range(2):
            source = self.shards[phase].at[:, self.columns(phase, half)]
            for flow in range(2):
                if half in self.halves(1, flow):
                    self.send(self.ring_copy(source, self.me, phase, 1, half, flow))
            self.send(self.core_copy(source, self.me, phase, 0, half))
            self.place(phase, half, self.me)[...] = source[...]

    def arrive(self, phase, step, half, flow):
        slot = self.device_at((2 * flow - 1) * step)
        arrived = self.place(phase, half, slot)
        self.ring_copy(arrived, slot, phase, step, half, flow).wait_recv()
        if step < self.reach and half in self.halves(step + 1, flow):
            self.send(self.ring_copy(arrived, slot, phase, step + 1, half, flow))
        self.send(self.core_copy(arrived, slot, phase, 1 + flow * self.reach + step - 1, half))

    def tick(self, count=1):
        for _ in range(count):
            if self.taken < len(self.steps):
                self.steps[self.taken]()
                self.taken += 1

    def need(self, phase):
        self.tick(max(0, self.ends[phase] - self.taken))
        for half in range(2):
            slot = self.partner
            self.core_copy(self.place(phase, half, slot), slot, phase, 0, half).wait_recv()
            for step in range(1, self.reach + 1):
                for flow in range(2):
                    if half in self.halves(step, flow):
                        slot = self.device_at((2 * flow - 1) * step, 1 - self.core)
                        self.core_copy(
                            self.place(phase, half, slot),
                            slot,
                            phase,
                            1 + flow * self.reach + step - 1,
                            half,
                        ).wait_recv()

    def finish(self):
        for copy in self.sends:
            copy.wait_send()


CHUNKS = 4


def forward_kernel(widths, n, in_shard, out_shard, rows_in, heads, same, masks, *rest):
    count = len(ACTS)
    wholes_out, rest = rest[:4], rest[4:]
    stream_0, stream_1, total_0, inv_0, part_1, inv_1 = rest[:6]
    acts = named(rest[6 : 6 + count]), named(rest[6 + count : 6 + 2 * count])
    (
        *wholes, part_0, other_0, square_0, other_square, square_1, other_square_1, ring_send, ring_recv, core_send,
        core_recv, pair_send, pair_recv, out_sem
    ) = rest[6 + 2 * count :]
    shards = (in_shard.at[0], out_shard.at[0], in_shard.at[1], out_shard.at[1])
    gather = Gather(n, shards, wholes, ring_send, ring_recv, core_send, core_recv)
    across = 1 - lax.axis_index("tensor")
    barrier = pltpu.get_barrier_semaphore()
    for target in (*gather.sides, gather.partner):
        pl.semaphore_signal(barrier, inc=1, device_id={"dp": target}, device_id_type=MESH)
    pl.semaphore_signal(barrier, inc=1, device_id={"tensor": across}, device_id_type=MESH)
    pl.semaphore_wait(barrier, 4)
    gather.tick(len(GROUPS[0]))
    stream_0[...] = live_of(rows_in, masks)
    outs = []

    def need(phase):
        gather.need(phase)
        outs.append(
            pltpu.make_async_copy(wholes[phase], wholes_out[phase], out_sem.at[phase])
        )
        outs[-1].start()

    copies = []

    def send_square(square):
        square_0[...] = square
        copies.append(
            remote(
                square_0, other_square, pair_send.at[CHUNKS], pair_recv.at[CHUNKS], across, "tensor"
            )
        )
        copies[-1].start()

    def send_part(chunk, columns, values):
        part_0[:, columns] = values
        copies.append(
            remote(
                part_0.at[:, columns],
                other_0.at[:, columns],
                pair_send.at[chunk],
                pair_recv.at[chunk],
                across,
                "tensor",
            )
        )
        copies[-1].start()

    need(0)
    forward_part(
        stream_0[...], wholes[0], wholes[1], heads.at[0], same, masks, acts[0], widths, n,
        gather.tick, functools.partial(need, 1), send_square, send_part
    )
    gather.tick(2)
    for copy in copies:
        copy.wait()
    total_0[...], scale = mixed_of(part_0[...], other_0[...], square_0[...], other_square[...])
    inv_0[...] = jnp.broadcast_to(scale, inv_0.shape)
    stream_1[...] = stream_0[...] + total_0[...] * scale
    need(2)

    late = remote(
        square_1, other_square_1, pair_send.at[CHUNKS + 1], pair_recv.at[CHUNKS + 1], across, "tensor"
    )

    def keep_square(square):
        square_1[...] = square
        late.start()

    def keep_part(chunk, columns, values):
        part_1[:, columns] = values

    forward_part(
        stream_1[...], wholes[2], wholes[3], heads.at[1], same, masks, acts[1], widths, n,
        gather.tick, functools.partial(need, 3), keep_square, keep_part
    )
    gather.finish()
    late.wait()
    scale = lax.rsqrt((square_1[...] + other_square_1[...])[:, 0:1] / E + EPSILON)
    inv_1[...] = jnp.broadcast_to(scale, inv_1.shape)
    for copy in outs:
        copy.wait()


def gather_forward(in_shard, out_shard, rows_in, heads, same, masks, widths, n):
    shard = in_shard.shape[1]
    reach = n // 4
    rows, model = rows_in.shape
    wholes = [
        shape(n * shard, array.shape[2], BF16)
        for array in (in_shard, out_shard, in_shard, out_shard)
    ]
    acts = act_shapes(model, widths)
    outs = [
        shape(rows, model, F32),
        shape(rows, model, F32),
        shape(rows, model, F32),
        shape(rows, SMALL, F32),
        shape(rows, model, BF16),
        shape(rows, SMALL, F32),
    ]
    vmem = pl.BlockSpec(memory_space=pltpu.VMEM)
    results = pl.pallas_call(
        functools.partial(forward_kernel, widths, n),
        out_shape=(*wholes, *outs, *acts, *acts),
        in_specs=[vmem] * 6,
        out_specs=(pl.BlockSpec(memory_space=pl.ANY),) * 4 + (vmem,) * (6 + 2 * len(acts)),
        scratch_shapes=[pltpu.VMEM(whole.shape, BF16) for whole in wholes]
        + [
            pltpu.VMEM((rows, model), BF16),
            pltpu.VMEM((rows, model), BF16),
            pltpu.VMEM((rows, SMALL), F32),
            pltpu.VMEM((rows, SMALL), F32),
            pltpu.VMEM((rows, SMALL), F32),
            pltpu.VMEM((rows, SMALL), F32),
            pltpu.SemaphoreType.DMA((2, reach, 8)),
            pltpu.SemaphoreType.DMA((2, reach, 8)),
            pltpu.SemaphoreType.DMA((2 * reach + 1, 8)),
            pltpu.SemaphoreType.DMA((2 * reach + 1, 8)),
            pltpu.SemaphoreType.DMA((CHUNKS + 2,)),
            pltpu.SemaphoreType.DMA((CHUNKS + 2,)),
            pltpu.SemaphoreType.DMA((4,)),
        ],
        compiler_params=pltpu.CompilerParams(
            collective_id=0, has_side_effects=True, vmem_limit_bytes=60 * 1024 * 1024
        ),
        name="gather_forward",
    )(in_shard, out_shard, rows_in, heads, same, masks)
    count = len(acts)
    return results[:4], results[4:10], results[10 : 10 + count], results[10 + count :]


F32 = jnp.float32
BF16 = jnp.bfloat16
VROWS = 16
NN = (((1,), (0,)), ((), ()))
NT = (((1,), (1,)), ((), ()))
TN = (((0,), (0,)), ((), ()))


def mul(a, b, dims=NN):
    return lax.dot_general(
        a.astype(BF16), b.astype(BF16), dims, preferred_element_type=F32
    )


def mul_wide(a, b, dims=NN):
    return lax.dot_general(a, b, dims, precision=HIGHEST, preferred_element_type=F32)


def mul_split(a, b, dims=NN):
    high = a.astype(BF16)
    low = (a - high.astype(F32)).astype(BF16)
    return mul(high, b, dims) + mul(low, b, dims)


def iota(shape, axis):
    return lax.broadcasted_iota(jnp.int32, shape, axis)


def one_hot(mask):
    return jnp.where(mask, 1.0, 0.0).astype(BF16)


def row_picker(head_count):
    shape = (VROWS, SMALL)
    return one_hot(iota(shape, 0) + head_count == iota(shape, 1))


def state_picker(model, state_width, n):
    per_device = state_width // n
    shape = (model, state_width)
    column = iota(shape, 1)
    owner = lax.shift_right_logical(column, per_device.bit_length() - 1)
    return one_hot(
        iota(shape, 0) == owner * (model // n) + jnp.bitwise_and(column, per_device - 1)
    )


def head_picker(inner_width, head_count):
    head_size = inner_width // head_count
    shape = (inner_width, SMALL)
    return one_hot(
        lax.shift_right_logical(iota(shape, 0), head_size.bit_length() - 1) == iota(shape, 1)
    )


def slope_of(values):
    sigmoid_val = jax.nn.sigmoid(values)
    return sigmoid_val * (1.0 + values * (1.0 - sigmoid_val))


def softplus(values):
    return jnp.maximum(values, 0.0) + jnp.log1p(jnp.exp(-jnp.abs(values)))


def causal_conv(raw, taps, bias, masks):
    total = bias + taps[KERNEL - 1 : KERNEL] * raw
    for lag in range(1, KERNEL):
        tap = KERNEL - 1 - lag
        total = total + taps[tap : tap + 1] * (pltpu.roll(raw, lag, 0) * masks[:, lag : lag + 1])
    return total


def causal_conv_back(grad, raw, taps, masks):
    rows = grad.shape[0]
    tap_grads = [None] * KERNEL
    tap_grads[KERNEL - 1] = jnp.sum(grad * raw, axis=0, keepdims=True)
    source = taps[KERNEL - 1 : KERNEL] * grad
    for lag in range(1, KERNEL):
        tap = KERNEL - 1 - lag
        masked = grad * masks[:, lag : lag + 1]
        tap_grads[tap] = jnp.sum(masked * pltpu.roll(raw, lag, 0), axis=0, keepdims=True)
        source = source + taps[tap : tap + 1] * pltpu.roll(masked, rows - lag, 0)
    return tap_grads + [jnp.sum(grad, axis=0, keepdims=True)], source


def row_scale(stream):
    return lax.rsqrt(jnp.mean(stream * stream, axis=1, keepdims=True) + EPSILON)


def pair_blocks(head_count, inner_width):
    head_size = inner_width // head_count
    per_block = SMALL // head_size
    return [
        (slice(block * SMALL, (block + 1) * SMALL), range(block * per_block, (block + 1) * per_block))
        for block in range(inner_width // SMALL)
    ]


def spread(columns, heads, head_size):
    rows = columns.shape[0]
    lane_head = lax.shift_right_logical(iota((rows, SMALL), 1), head_size.bit_length() - 1)
    total = columns[:, heads[0] : heads[0] + 1]
    for place in range(1, len(heads)):
        total = jnp.where(lane_head >= place, columns[:, heads[place] : heads[place] + 1], total)
    return jnp.broadcast_to(total, (rows, SMALL))


def head_lanes(rows, head_size, place):
    lane_head = lax.shift_right_logical(iota((rows, SMALL), 1), head_size.bit_length() - 1)
    return lane_head == place


def decay_of(cum, cum_t, head, inside):
    diff = cum[:, head : head + 1] - cum_t[head : head + 1, :]
    return jnp.exp(jnp.where(inside, diff, -1e30))


ACTS = (
    ("normed", BF16, "model"),
    ("gate_pre", F32, "inner"),
    ("inner_raw", F32, "inner"),
    ("inner_pre", F32, "inner"),
    ("ssm", F32, "inner"),
    ("state_raw", F32, "state"),
    ("state_pre", F32, "state"),
    ("step_raw", F32, "small"),
    ("cum", F32, "small"),
    ("vec", F32, "model"),
    ("vec_state", F32, "state"),
)


def act_shapes(model, widths):
    inner_width, state_width, _ = widths
    width_of = {"model": model, "inner": inner_width, "state": state_width, "small": SMALL}
    return [
        jax.ShapeDtypeStruct(
            (VROWS if name.startswith("vec") else BAL, width_of[kind]), dtype
        )
        for name, dtype, kind in ACTS
    ]


def named(refs):
    return dict(zip([name for name, _, _ in ACTS], refs))


def forward_part(
    stream, w_in, w_out, head_ref, same_ref, mask_ref, acts, widths, n, tick, need_out, on_square,
    on_part
):
    inner_width, state_width, head_count = widths
    model = stream.shape[1]
    rows = stream.shape[0]
    head_size = inner_width // head_count
    half = state_width // 2
    at_state = 2 * inner_width
    at_small = at_state + state_width
    masks = mask_ref[...]
    inside = same_ref[...] > 0.5
    vec = mul(row_picker(head_count), w_in[:, at_small : at_small + SMALL], NT)
    vec_state = mul(vec, state_picker(model, state_width, n))
    acts["vec"][...] = vec
    acts["vec_state"][...] = vec_state
    normed = (stream * row_scale(stream) * vec[0:1]).astype(BF16)
    acts["normed"][...] = normed
    state_step = mul(normed, w_in[:, at_state : at_small + SMALL])
    state_raw = state_step[:, :state_width]
    step_raw = state_step[:, state_width:] + head_ref[0:1]
    acts["state_raw"][...] = state_raw
    acts["step_raw"][...] = step_raw
    tick()
    state_pre = causal_conv(state_raw, vec_state[7:11], vec_state[11:12], masks)
    acts["state_pre"][...] = state_pre
    state = state_pre * jax.nn.sigmoid(state_pre)
    step = softplus(step_raw)
    rate = -jnp.exp(head_ref[1:2])
    cum = mul_wide(same_ref[...], step * rate)
    acts["cum"][...] = cum
    cum_t = cum.T
    intersection = mul(state[:, half:], state[:, :half], NT)
    tick()
    inner_raw = mul(normed, w_in[:, inner_width:at_state])
    acts["inner_raw"][...] = inner_raw
    inner_pre = causal_conv(inner_raw, vec[1:5], vec[5:6], masks)
    acts["inner_pre"][...] = inner_pre
    tick()
    gate_pre = mul(normed, w_in[:, :inner_width])
    acts["gate_pre"][...] = gate_pre
    skip = head_ref[2:3]
    pieces = []
    square = jnp.zeros((rows, 1), F32)
    for block, (lanes, heads) in enumerate(pair_blocks(head_count, inner_width)):
        if block % 2 == 0:
            tick()
        pre = inner_pre[:, lanes]
        inner = pre * jax.nn.sigmoid(pre)
        scaled = (inner * spread(step, heads, head_size)).astype(BF16)
        out = spread(skip, heads, head_size) * inner
        for place, head in enumerate(heads):
            mixer = decay_of(cum, cum_t, head, inside) * intersection
            out = out + jnp.where(head_lanes(rows, head_size, place), mul(mixer, scaled), 0.0)
        acts["ssm"][:, lanes] = out
        gate = gate_pre[:, lanes]
        gated = out * gate * jax.nn.sigmoid(gate)
        square = square + jnp.sum(gated * gated, axis=1, keepdims=True)
        pieces.append((gated * vec[6:7, lanes]).astype(BF16))
    on_square(jnp.broadcast_to(square, (rows, SMALL)))
    need_out()
    gated_low = jnp.concatenate(pieces, axis=1)
    for chunk in range(CHUNKS):
        columns = slice(chunk * model // CHUNKS, (chunk + 1) * model // CHUNKS)
        on_part(chunk, columns, mul(gated_low, w_out[columns], NT).astype(BF16))


def mixed_of(part, other, square, other_square):
    total = part.astype(F32) + other.astype(F32)
    return total, lax.rsqrt((square + other_square)[:, 0:1] / E + EPSILON)


def backward_part(
    grad, scale, total_of, w_in, w_out, head_ref, same_ref, mask_ref, acts, joined_ref, turn_ref,
    gated_ref, grad_in, grad_out, grad_small, vec_grads, widths, n, tick, need_out, need_in,
    on_out, on_part, on_in, on_heads
):
    inner_width, state_width, head_count = widths
    rows, model = grad.shape
    shard = grad_in.shape[1]
    head_size = inner_width // head_count
    half = state_width // 2
    at_state = 2 * inner_width
    at_small = at_state + state_width
    per = SMALL // shard
    masks = mask_ref[...]
    inside = same_ref[...] > 0.5
    vec = acts["vec"][...]
    vec_state = acts["vec_state"][...]
    grad_low = grad.astype(BF16)
    turn_ref[...] = grad.T.astype(BF16)
    for lanes, _ in pair_blocks(head_count, inner_width):
        gate = acts["gate_pre"][:, lanes]
        gated = acts["ssm"][:, lanes] * gate * jax.nn.sigmoid(gate)
        gated_ref[:, lanes] = (gated * scale * vec[6:7, lanes]).astype(BF16)
    for block in range(model // SMALL):
        mine = slice(block * SMALL, (block + 1) * SMALL)
        grad_out[block * per : (block + 1) * per] = (
            mul(turn_ref[mine], gated_ref[...]).reshape(per, shard, inner_width).astype(BF16)
        )
    on_out()
    tick()
    need_out()
    d_gate_normed = mul(grad_low, w_out[...])
    tick()
    step_raw = acts["step_raw"][...]
    step = softplus(step_raw)
    rate = -jnp.exp(head_ref[1:2])
    skip = head_ref[2:3]
    cum = acts["cum"][...]
    cum_t = cum.T
    state_pre = acts["state_pre"][...]
    state = state_pre * jax.nn.sigmoid(state_pre)
    intersection = mul(state[:, half:], state[:, :half], NT)
    inner_sum = jnp.sum(grad_low.astype(F32) * total_of(), axis=1, keepdims=True)
    pull = scale * scale * scale * inner_sum / E
    d_intersection = jnp.zeros((rows, rows), F32)
    row_part = jnp.zeros((rows, SMALL), F32)
    column_part = jnp.zeros((SMALL, rows), F32)
    head_lane = iota((rows, SMALL), 1)
    head_row = iota((SMALL, rows), 0)
    gain_grads = []
    skip_parts = []
    step_parts = []
    inner_taps = []
    for lanes, heads in pair_blocks(head_count, inner_width):
        tick()
        pre = acts["inner_pre"][:, lanes]
        sigmoid_inner = jax.nn.sigmoid(pre)
        inner = pre * sigmoid_inner
        gate = acts["gate_pre"][:, lanes]
        gate_sig = jax.nn.sigmoid(gate)
        ssm = acts["ssm"][:, lanes]
        act = gate * gate_sig
        gated = ssm * act
        gain = vec[6:7, lanes]
        d_normed = d_gate_normed[:, lanes]
        gain_grads.append(jnp.sum(d_normed * gated * scale, axis=0, keepdims=True))
        d_gated = scale * gain * d_normed - gated * pull
        d_ssm = d_gated * act
        joined_ref[:, lanes] = (
            d_gated * ssm * gate_sig * (1.0 + gate * (1.0 - gate_sig))
        ).astype(BF16)
        skip_parts.append(jnp.sum(d_ssm * inner, axis=0, keepdims=True))
        step_wide = spread(step, heads, head_size)
        scaled = (inner * step_wide).astype(BF16)
        d_low = d_ssm.astype(BF16)
        d_scaled = jnp.zeros((rows, SMALL), F32)
        for place, head in enumerate(heads):
            mine = head_lanes(rows, head_size, place)
            decay = decay_of(cum, cum_t, head, inside)
            mixer = decay * intersection
            d_scaled = d_scaled + jnp.where(mine, mul(mixer, d_low, TN), 0.0)
            d_mixer = mul(jnp.where(mine, d_ssm, 0.0), scaled, NT)
            d_decayed = d_mixer * decay
            d_intersection = d_intersection + d_decayed
            flow = d_decayed * intersection
            row_part = jnp.where(
                head_lane == head, jnp.sum(flow, axis=1, keepdims=True), row_part
            )
            column_part = jnp.where(
                head_row == head, jnp.sum(flow, axis=0, keepdims=True), column_part
            )
        step_parts.append(d_scaled * inner)
        d_inner = spread(skip, heads, head_size) * d_ssm + d_scaled * step_wide
        d_pre = d_inner * (sigmoid_inner * (1.0 + pre * (1.0 - sigmoid_inner)))
        taps, d_raw = causal_conv_back(
            d_pre, acts["inner_raw"][:, lanes], vec[1:5, lanes], masks
        )
        inner_taps.append(taps)
        joined_ref[:, slice(inner_width + lanes.start, inner_width + lanes.stop)] = d_raw.astype(
            BF16
        )
    tick()
    d_log = mul_wide(same_ref[...], row_part - column_part.T, TN)
    picker = head_picker(inner_width, head_count)
    d_step = mul_split(jnp.concatenate(step_parts, axis=1), picker) + d_log * rate
    d_step_raw = jnp.where(head_lane < head_count, d_step * jax.nn.sigmoid(step_raw), 0.0)
    joined_ref[:, at_small : at_small + SMALL] = d_step_raw.astype(BF16)
    d_state = jnp.concatenate(
        [mul(d_intersection, state[:, half:], TN), mul(d_intersection, state[:, :half])], axis=1
    )
    state_taps, d_state_raw = causal_conv_back(
        d_state * slope_of(state_pre), acts["state_raw"][...], vec_state[7:11], masks
    )
    joined_ref[:, at_state:at_small] = d_state_raw.astype(BF16)
    tick()
    need_in()
    for chunk in range(CHUNKS):
        columns = slice(chunk * model // CHUNKS, (chunk + 1) * model // CHUNKS)
        on_part(chunk, columns, mul(joined_ref[...], w_in[columns], NT).astype(BF16))
    turn_ref[...] = acts["normed"][...].astype(F32).T.astype(BF16)
    for block in range(model // SMALL):
        if block % 2 == 0:
            tick()
        mine = slice(block * SMALL, (block + 1) * SMALL)
        product = mul(turn_ref[mine], joined_ref[...])
        grad_in[block * per : (block + 1) * per] = (
            product[:, :at_small].reshape(per, shard, at_small).astype(BF16)
        )
        grad_small[mine] = product[:, at_small:]
    on_in()
    skip_row = jnp.broadcast_to(jnp.concatenate(skip_parts, axis=1), (8, inner_width))
    on_heads(
        (
            jnp.sum(d_step_raw, axis=0, keepdims=True),
            jnp.sum(d_log * step, axis=0, keepdims=True) * rate,
            mul_split(skip_row, picker)[0:1],
        )
    )
    state_rows = jnp.concatenate(
        [jnp.zeros((7, state_width), F32)]
        + state_taps
        + [jnp.zeros((VROWS - 12, state_width), F32)]
    )
    vec_grads[...] = mul(state_rows, state_picker(model, state_width, n), NT)
    vec_grads[1:7] = jnp.concatenate(
        [
            jnp.concatenate([taps[row] for taps in inner_taps], axis=1)
            for row in range(KERNEL + 1)
        ]
        + [jnp.concatenate(gain_grads, axis=1)]
    )


def finish_part(d_normed, grad, stream, acts, vec_grads, grad_small, small_out, head_count, shard):
    model = stream.shape[1]
    inv_rms = row_scale(stream)
    vec_grads[0:1] = jnp.sum(d_normed * stream * inv_rms, axis=0, keepdims=True)
    small = grad_small[...] + mul(vec_grads[...], row_picker(head_count), TN)
    small_out[...] = small.reshape(model // shard, shard, SMALL).astype(BF16)
    scaled = d_normed * acts["vec"][0:1]
    return (
        grad
        + inv_rms * scaled
        - stream
        * (inv_rms * inv_rms * inv_rms)
        * jnp.sum(scaled * stream, axis=1, keepdims=True)
        / model
    )


def running_sum(lengths):
    index = jnp.arange(lengths.shape[0], dtype=jnp.int32)
    return jnp.sum(jnp.where(index[:, None] >= index[None, :], lengths[None, :], 0), axis=1)


def segments_of(lengths, row_total):
    ends = running_sum(lengths)
    position = jnp.arange(row_total, dtype=jnp.int32)
    return jnp.sum((position[:, None] >= ends[None, :]).astype(jnp.int32), axis=1)


def seq_structure(segment_ids):
    row_total = segment_ids.shape[0]
    position = jnp.arange(row_total, dtype=jnp.int32)
    same_seq = (
        (segment_ids[:, None] == segment_ids[None, :]) & (position[:, None] >= position[None, :])
    ).astype(jnp.float32)
    conv_masks = [None]
    for lag_rows in range(1, KERNEL):
        earlier = jnp.concatenate([jnp.full((lag_rows,), -1, jnp.int32), segment_ids[:-lag_rows]])
        conv_masks.append((segment_ids == earlier).astype(jnp.float32)[:, None])
    return (same_seq, conv_masks)


def take_rows(buffer, start_row, row_count):
    padding = jnp.zeros((row_count, buffer.shape[1]), buffer.dtype)
    return lax.dynamic_slice_in_dim(
        jnp.concatenate([buffer, padding], axis=0), start_row, row_count, 0
    )


def place_rows(own_rows, arrived, kept_rows, rows_out):
    row_width = own_rows.shape[1]
    if own_rows.shape[0] >= rows_out:
        base_rows = own_rows[:rows_out]
    else:
        base_rows = jnp.concatenate(
            [own_rows, jnp.zeros((rows_out - own_rows.shape[0], row_width), own_rows.dtype)], axis=0
        )
    extended = jnp.concatenate(
        [
            jnp.zeros((rows_out, row_width), own_rows.dtype),
            arrived,
            jnp.zeros((rows_out - arrived.shape[0], row_width), own_rows.dtype),
        ],
        axis=0,
    )
    moved_rows = lax.dynamic_slice_in_dim(extended, rows_out - kept_rows, rows_out, 0)
    position = jnp.arange(rows_out, dtype=jnp.int32)
    return jnp.where((position < kept_rows)[:, None], base_rows, moved_rows)


def balanced_layout(own_len, partner_len):
    own_end = running_sum(own_len)
    keep_flag = (own_end <= BAL).astype(jnp.int32)
    kept_rows = jnp.sum(own_len * keep_flag)
    partner_end = running_sum(partner_len)
    incoming = partner_len * (partner_end > BAL).astype(jnp.int32)
    segment_ids = segments_of(jnp.concatenate([own_len * keep_flag, incoming]), BAL)
    live_rows = (jnp.arange(BAL, dtype=jnp.int32) < kept_rows + jnp.sum(incoming))[:, None]
    return (segment_ids, live_rows, kept_rows)


def pad_rows(array, rows):
    return jnp.pad(array, ((0, 0), (0, rows - array.shape[1]), (0, 0)))


def pack_weights(stacked):
    (
        gate_inner_proj,
        step_proj,
        state_proj,
        conv_inner,
        conv_inner_bias,
        conv_state,
        conv_state_bias,
        norm_gain,
        gate_gain,
        out_proj,
    ) = stacked
    layers, rows = norm_gain.shape
    columns = [
        step_proj,
        norm_gain[:, :, None],
        jnp.swapaxes(conv_inner, 1, 2),
        conv_inner_bias[:, :, None],
        gate_gain[:, :, None],
        pad_rows(jnp.swapaxes(conv_state, 1, 2), rows),
        pad_rows(conv_state_bias[:, :, None], rows),
    ]
    used = sum(column.shape[2] for column in columns)
    columns.append(jnp.zeros((layers, rows, SMALL - used), norm_gain.dtype))
    in_shard = jnp.concatenate(
        [gate_inner_proj.reshape(layers, rows, -1), state_proj] + columns, axis=2
    )
    return in_shard, jnp.swapaxes(out_proj, 1, 2)


def unpack_grads(total, widths, n):
    inner_width, state_width, head_count = widths
    layers, rows = total.shape[:2]
    in_width = 2 * inner_width + state_width
    per_device = state_width // n
    small = total[:, :, total.shape[2] - SMALL :]
    step = small[:, :, :head_count]
    small = small[:, :, head_count : head_count + 12]
    shared = jnp.concatenate(
        [total[:, :, 2 * inner_width : in_width], jnp.pad(small[:, :, 7:12], ((0, 0), (0, 0), (0, SMALL - 5)))],
        axis=2,
    )
    shared = shared + swapped(shared, "tensor", 0)
    state = shared[:, :per_device, state_width:]
    return (
        total[:, :, : 2 * inner_width].reshape(layers, rows, 2, inner_width),
        step,
        shared[:, :, :state_width],
        jnp.swapaxes(small[:, :, 1:5], 1, 2),
        small[:, :, 5],
        jnp.swapaxes(state[:, :, :KERNEL], 1, 2),
        state[:, :, KERNEL],
        small[:, :, 0],
        small[:, :, 6],
        jnp.swapaxes(total[:, :, in_width : total.shape[2] - SMALL], 1, 2),
    )


def shape(rows, columns, dtype):
    return jax.ShapeDtypeStruct((rows, columns), dtype)


def live_of(values, mask_ref):
    return jnp.where(mask_ref[:, KERNEL : KERNEL + 1] > 0.5, values[...].astype(F32), 0.0)


ROUNDS = (2, 6, 10, 14, 18, 22, 26, 30)


class Scatter:
    def __init__(self, n, widths, grads, core_bufs, recv_bufs, out_ref, sems):
        inner_width, state_width, _ = widths
        self.n = n
        self.chips = n // 2
        self.me, self.core, self.position = ring_place(self.chips)
        self.partner = self.me + 1 - 2 * self.core
        self.sides = tuple(
            ring_chip(self.position + offset, self.chips) * 2 + self.core for offset in (1, -1)
        )
        self.grads, self.core_bufs, self.recv_bufs = grads, core_bufs, recv_bufs
        self.out_ref = out_ref
        self.core_send, self.core_recv, self.ring_send, self.ring_recv = sems
        in_width = 2 * inner_width + state_width
        self.places = (0, in_width, in_width + inner_width)
        self.cuts = (in_width // (2 * SMALL) * SMALL, inner_width // (2 * SMALL) * SMALL, 0)
        self.sizes = (in_width, inner_width, SMALL)
        self.sends = []
        self.streams = []
        self.turn = 0

    def parts(self, layer, array):
        if array == 2:
            return [(4, layer, 0, SMALL)]
        cut = self.cuts[array]
        return [
            (2 * array, 0, 0, cut),
            (2 * array + 1, 1, cut, self.sizes[array] - cut),
        ]

    def chip_at(self, flow, step):
        return ring_chip(self.position + (2 * flow - 1) * step, self.chips)

    def core_copy(self, layer, array, part, step):
        index, flow, start, size = part
        return remote(
            self.grads[layer][array].at[
                2 * self.chip_at(flow, step) + 1 - self.core, :, pl.ds(start, size)
            ],
            self.core_bufs[layer].at[step - 1, :, pl.ds(self.places[array] + start, size)],
            self.core_send.at[layer, step - 1, index],
            self.core_recv.at[layer, step - 1, index],
            self.partner,
        )

    def ring_copy(self, layer, array, part, step):
        index, flow, start, size = part
        return remote(
            self.grads[layer][array].at[
                2 * self.chip_at(flow, step) + self.core, :, pl.ds(start, size)
            ],
            self.recv_bufs[layer].at[step - 1, :, pl.ds(self.places[array] + start, size)],
            self.ring_send.at[layer, step - 1, index],
            self.ring_recv.at[layer, step - 1, index],
            self.sides[flow],
        )

    def begin(self, layer, array):
        for step in range(1, self.chips + 1):
            for part in self.parts(layer, array):
                self.send(self.core_copy(layer, array, part, step))
        self.streams.append(
            [
                functools.partial(self.advance, layer, array, step)
                for step in range(1, self.chips + 1)
            ]
        )

    def send(self, copy):
        copy.start()
        self.sends.append(copy)

    def advance(self, layer, array, step):
        for part in self.parts(layer, array):
            _, flow, start, size = part
            place = pl.ds(self.places[array] + start, size)
            own = 2 * self.chip_at(flow, step) + self.core
            self.core_copy(layer, array, part, step).wait_recv()
            total = self.grads[layer][array][own, :, pl.ds(start, size)].astype(F32)
            total = total + self.core_bufs[layer][step - 1, :, place].astype(F32)
            if step > 1:
                self.ring_copy(layer, array, part, step - 1).wait_recv()
                total = total + self.recv_bufs[layer][step - 2, :, place].astype(F32)
            if step == self.chips:
                self.out_ref[layer, :, place] = total
            else:
                self.grads[layer][array][own, :, pl.ds(start, size)] = total.astype(BF16)
                self.send(self.ring_copy(layer, array, part, step))

    def tick(self):
        if self.turn in ROUNDS:
            self.round()
        self.turn += 1

    def round(self):
        for stream in self.streams:
            if stream:
                stream.pop(0)()

    def drain(self):
        while any(self.streams):
            self.round()

    def finish(self):
        for copy in self.sends:
            copy.wait_send()


def backward_kernel(
    widths, n, in_1, out_1, in_0, out_0, part_1, inv_1, stream_1, stream_0, total_0, inv_0,
    cotan, heads, same, masks, *rest
):
    count = len(ACTS)
    acts = named(rest[count : 2 * count]), named(rest[:count])
    acts = acts[::-1]
    rest = rest[2 * count :]
    result, gradient, out_ref, heads_ref = rest[:4]
    (
        w_in_1, w_out_1, w_in_0, w_out_0, grad_in_1, grad_out_1, grad_small_1, grad_in_0, grad_out_0,
        grad_small_0, core_1, core_0, recv_1, recv_0, joined, turn, gated, small, vec_grads,
        head_block, other_part, send_0, send_1, arrive_0, arrive_1, grad_1, core_send,
        core_recv, ring_send, ring_recv, head_send, head_recv, pair_send, pair_recv, weight_sem
    ) = rest[4:]
    loads = [
        pltpu.make_async_copy(source, target, weight_sem.at[index])
        for index, (source, target) in enumerate(
            ((out_1, w_out_1), (in_1, w_in_1), (out_0, w_out_0), (in_0, w_in_0))
        )
    ]
    for load in loads:
        load.start()
    scatter = Scatter(
        n,
        widths,
        ((grad_in_0, grad_out_0, grad_small_0), (grad_in_1, grad_out_1, grad_small_1)),
        (core_0, core_1),
        (recv_0, recv_1),
        out_ref,
        (core_send, core_recv, ring_send, ring_recv),
    )
    me = scatter.me
    across = 1 - lax.axis_index("tensor")
    barrier = pltpu.get_barrier_semaphore()

    @pl.loop(1, n)
    def _(k):
        pl.semaphore_signal(
            barrier, inc=1, device_id={"dp": lax.rem(me + k, n)}, device_id_type=MESH
        )

    pl.semaphore_signal(barrier, inc=1, device_id={"tensor": across}, device_id_type=MESH)
    pl.semaphore_wait(barrier, n)

    def pair_copy(source, target, index):
        return remote(
            source, target, pair_send.at[index], pair_recv.at[index], across, "tensor"
        )

    part_copy = pair_copy(part_1, other_part, 0)
    part_copy.start()
    head_block[...] = jnp.zeros(head_block.shape, F32)

    def layer_of(layer, grad, scale, total_of, w_in, w_out, sent, arrived, loaded):
        copies = []

        def on_part(chunk, columns, values):
            sent[:, columns] = values
            copies.append(
                pair_copy(
                    sent.at[:, columns], arrived.at[:, columns], 1 + CHUNKS * layer + chunk
                )
            )
            copies[-1].start()

        def on_heads(grads):
            for row, values in enumerate(grads):
                head_block[3 * layer + row : 3 * layer + row + 1] = values

        backward_part(
            grad, scale, total_of, w_in, w_out, heads.at[layer], same, masks, acts[layer], joined,
            turn, gated, scatter.grads[layer][0], scatter.grads[layer][1], small, vec_grads, widths,
            n, scatter.tick, loads[loaded].wait, loads[loaded + 1].wait,
            functools.partial(scatter.begin, layer, 1), on_part,
            functools.partial(scatter.begin, layer, 0), on_heads
        )
        scatter.tick()
        for copy in copies:
            copy.wait()
        return sent[...].astype(F32) + arrived[...].astype(F32)

    scale_1 = inv_1[:, 0:1]

    def total_1():
        part_copy.wait()
        total = part_1[...].astype(F32) + other_part[...].astype(F32)
        result[...] = (stream_1[...] + total * scale_1).astype(BF16)
        return total

    last_grad = live_of(cotan, masks)
    d_normed = layer_of(
        1, last_grad, scale_1, total_1, w_in_1, w_out_1, send_1, arrive_1, 0
    )
    grad_1[...] = finish_part(
        d_normed, last_grad, stream_1[...], acts[1], vec_grads, small, grad_small_1, widths[2],
        grad_small_1.shape[1]
    )
    scatter.begin(1, 2)
    d_normed = layer_of(
        0, grad_1[...], inv_0[:, 0:1], lambda: total_0[...], w_in_0, w_out_0, send_0, arrive_0, 2
    )

    def head_copy(k, place):
        return remote(
            head_block,
            heads_ref.at[place],
            head_send.at[k],
            head_recv.at[k],
            lax.rem(me + k, n),
        )

    @pl.loop(1, n)
    def _(k):
        head_copy(k, me).start()

    heads_ref[pl.ds(me, 1)] = head_block[...][None]
    gradient[...] = finish_part(
        d_normed, grad_1[...], stream_0[...], acts[0], vec_grads, small, grad_small_0, widths[2],
        grad_small_0.shape[1]
    ).astype(BF16)
    scatter.begin(0, 2)
    scatter.drain()
    scatter.finish()

    @pl.loop(1, n)
    def _(k):
        copy = head_copy(k, lax.rem(me - k + n, n))
        copy.wait_send()
        copy.wait_recv()


def backward_scatter(wholes, kept, cotan, heads, same, masks, acts_0, acts_1, widths, n):
    in_0, out_0, in_1, out_1 = wholes
    stream_0, stream_1, total_0, inv_0, part_1, inv_1 = kept
    inner_width, state_width, _ = widths
    rows, model = cotan.shape
    shard = model // n
    chips = n // 2
    in_width = 2 * inner_width + state_width
    width = in_width + inner_width + SMALL
    vmem = pl.BlockSpec(memory_space=pltpu.VMEM)
    hbm = pl.BlockSpec(memory_space=pl.ANY)
    grads = [
        pltpu.VMEM((n, shard, columns), BF16) for columns in (in_width, inner_width, SMALL)
    ]
    low = pltpu.VMEM((rows, model), BF16)
    return pl.pallas_call(
        functools.partial(backward_kernel, widths, n),
        out_shape=(
            shape(rows, model, BF16),
            shape(rows, model, BF16),
            jax.ShapeDtypeStruct((LAYERS, shard, width), F32),
            jax.ShapeDtypeStruct((n, 8, SMALL), F32),
        ),
        in_specs=[hbm] * 4 + [vmem] * (10 + 2 * len(ACTS)),
        out_specs=(vmem,) * 4,
        scratch_shapes=[pltpu.VMEM(whole.shape, BF16) for whole in (in_1, out_1, in_0, out_0)]
        + grads
        + grads
        + [pltpu.VMEM((chips, shard, width), BF16)] * 2
        + [pltpu.VMEM((chips - 1, shard, width), BF16)] * 2
        + [
            pltpu.VMEM((rows, in_width + SMALL), BF16),
            pltpu.VMEM((model, rows), BF16),
            pltpu.VMEM((rows, inner_width), BF16),
            pltpu.VMEM((model, SMALL), F32),
            pltpu.VMEM((VROWS, model), F32),
            pltpu.VMEM((8, SMALL), F32),
            low,
            low,
            low,
            low,
            low,
            pltpu.VMEM((rows, model), F32),
            pltpu.SemaphoreType.DMA((2, chips, 5)),
            pltpu.SemaphoreType.DMA((2, chips, 5)),
            pltpu.SemaphoreType.DMA((2, chips - 1, 5)),
            pltpu.SemaphoreType.DMA((2, chips - 1, 5)),
            pltpu.SemaphoreType.DMA((n,)),
            pltpu.SemaphoreType.DMA((n,)),
            pltpu.SemaphoreType.DMA((1 + 2 * CHUNKS,)),
            pltpu.SemaphoreType.DMA((1 + 2 * CHUNKS,)),
            pltpu.SemaphoreType.DMA((4,)),
        ],
        compiler_params=pltpu.CompilerParams(
            collective_id=1, has_side_effects=True, vmem_limit_bytes=63 * 1024 * 1024
        ),
        name="backward_scatter",
    )(
        in_1, out_1, in_0, out_0, part_1, inv_1, stream_1, stream_0, total_0, inv_0, cotan, heads,
        same, masks, *acts_0, *acts_1
    )


def run_blocks(stream_in, cotan_in, segment_ids, live_rows, stacked, head_params):
    same, conv_masks = seq_structure(segment_ids)
    masks = jnp.concatenate(
        [jnp.ones_like(conv_masks[1])] + conv_masks[1:] + [live_rows.astype(F32)], axis=1
    )
    masks = jnp.pad(masks, ((0, 0), (0, SMALL - masks.shape[1])))
    n = lax.axis_size("dp")
    widths = (stacked[0].shape[3], stacked[2].shape[2], stacked[1].shape[2])
    head_count = widths[2]
    head_rows = jnp.pad(
        jnp.stack(head_params, axis=1).astype(F32), ((0, 0), (0, 5), (0, SMALL - head_count))
    )
    wholes, kept_rows, acts_0, acts_1 = gather_forward(
        *pack_weights(stacked), stream_in, head_rows, same, masks, widths, n
    )
    result, gradient, total, head_parts = backward_scatter(
        wholes, kept_rows, cotan_in, head_rows, same, masks, acts_0, acts_1, widths, n
    )
    weight_grads = unpack_grads(total, widths, n)
    head_total = jnp.sum(head_parts, axis=0)[:6, :head_count].reshape(LAYERS, 3, head_count)
    head_grads = tuple(head_total[:, slot_index] for slot_index in range(3))
    return (result, gradient, weight_grads, head_grads)


def body(
    block_input,
    cotangent,
    seq_len,
    norm_gain,
    gate_inner_proj,
    step_proj,
    state_proj,
    conv_inner,
    conv_inner_bias,
    conv_state,
    conv_state_bias,
    step_bias,
    log_rate,
    skip_gain,
    gate_gain,
    out_proj,
):
    home_count = block_input.shape[0]
    own_total = jnp.sum(seq_len)
    live_home = (jnp.arange(home_count, dtype=jnp.int32) < own_total)[:, None]
    stacked = (
        gate_inner_proj,
        step_proj,
        state_proj,
        conv_inner,
        conv_inner_bias,
        conv_state,
        conv_state_bias,
        norm_gain,
        gate_gain,
        out_proj,
    )
    head_params = (step_bias, log_rate, skip_gain)
    partner_bit = lax.axis_size("dp").bit_length() - 2
    partner_len = swapped(seq_len, "dp", partner_bit)
    segment_ids, live_rows, kept_rows = balanced_layout(seq_len, partner_len)
    arrived = swapped(
        (take_rows(block_input, kept_rows, LMAX), take_rows(cotangent, kept_rows, LMAX)),
        "dp",
        partner_bit,
    )
    stream_in = place_rows(block_input, arrived[0], kept_rows, BAL)
    cotan_in = place_rows(cotangent, arrived[1], kept_rows, BAL)
    result, gradient, weight_grads, head_grads = run_blocks(
        stream_in, cotan_in, segment_ids, live_rows, stacked, head_params
    )
    out_rows, grad_rows = result, gradient
    returned = swapped(
        (take_rows(out_rows, kept_rows, LMAX), take_rows(grad_rows, kept_rows, LMAX)),
        "dp",
        partner_bit,
    )
    out_rows = place_rows(out_rows, returned[0], kept_rows, home_count)
    grad_rows = place_rows(grad_rows, returned[1], kept_rows, home_count)
    zero_rows = jnp.zeros_like(out_rows)
    out_rows = jnp.where(live_home, out_rows, zero_rows)
    grad_rows = jnp.where(live_home, grad_rows, zero_rows)
    return (
        out_rows,
        grad_rows,
        weight_grads[7],
        weight_grads[0],
        weight_grads[1],
        weight_grads[2],
        weight_grads[3],
        weight_grads[4],
        weight_grads[5],
        weight_grads[6],
        head_grads[0],
        head_grads[1],
        head_grads[2],
        weight_grads[8],
        weight_grads[9],
    )


def solution(mesh):
    return jax.shard_map(
        body,
        mesh=mesh,
        in_specs=(
            P("dp", None),
            P("dp", None),
            P("dp"),
            P(None, "dp"),
            P(None, "dp", None, "tensor"),
            P(None, "dp", "tensor"),
            P(None, "dp", None),
            P(None, None, ("tensor", "dp")),
            P(None, ("tensor", "dp")),
            P(None, None, "dp"),
            P(None, "dp"),
            P(None, "tensor"),
            P(None, "tensor"),
            P(None, "tensor"),
            P(None, ("tensor", "dp")),
            P(None, "tensor", "dp"),
        ),
        out_specs=(
            P("dp", None),
            P("dp", None),
            P(None, "dp"),
            P(None, "dp", None, "tensor"),
            P(None, "dp", "tensor"),
            P(None, "dp", None),
            P(None, None, ("tensor", "dp")),
            P(None, ("tensor", "dp")),
            P(None, None, "dp"),
            P(None, "dp"),
            P(None, "tensor"),
            P(None, "tensor"),
            P(None, "tensor"),
            P(None, ("tensor", "dp")),
            P(None, "tensor", "dp"),
        ),
        check_vma=False,
    )
```
